512 devices in a mesh: ctx: 64 (over z, y), tp: 8 (over x, core).
Axes of the slice: x: 4, y: 4, z: 16, core: 2. Of those that a mesh axis runs over, the one named last changes fastest.
Arguments:
- queries: bfloat16 [8192, 2048], P('ctx', 'tp'), may hold values from -6 to 6
- key_vectors: bfloat16 [8192, 2, 2048], P('ctx', None, 'tp'), may hold values from -40 to 40
- value_vectors: bfloat16 [8192, 2, 2048], P('ctx', None, 'tp'), may hold values from -40 to 40
- strengths: float32 [2, 16, 8192], P(None, 'tp', 'ctx'), may hold values from 0 to 2
- log_gate: float32 [16, 8192], P('tp', 'ctx'), may hold values from -2 to 0
- out_gain: float32 [2048], P('tp'), may hold values from 0.1 to 1.9
- out_weight: bfloat16 [2048, 4096], P('tp'), may hold values from -0.125 to 0.125
Outputs:
- layer_out: bfloat16 [8192, 4096], P('ctx', 'tp')
The draws below stay inside these ranges and needn't reach their ends.
All inputs are finite; a program needn't handle non-finite values.
Results may differ from the reference program's by a relative error of at most 0.019.
Values may be sent and summed in bfloat16 or wider, within the bound.
A program may use at most 64 MiB of HBM per device.

```python
import math
import jax
import jax.numpy as jnp
from jax import lax

D = 4096
RESIDENT_ATTNS = 16
DK = 128
DV = 128
TOK_DEV = 128
SPAN_ELEMENTS = 8192
N_TP = 8


def slow_heads(key):
    share = 0.5
    return jax.random.uniform(jax.random.fold_in(key, 7), (RESIDENT_ATTNS,)) < share


def multiplied_quantity(key, shape):
    noise_key, column_key, row_key = jax.random.split(key, 3)
    base = jax.random.truncated_normal(noise_key, -4.0, 4.0, shape)
    low = math.log(0.3)
    high = math.log(3.0)
    columns = jnp.exp(jax.random.uniform(column_key, (shape[2],), minval=low, maxval=high))
    row_scales = jnp.exp(jax.random.uniform(row_key, (shape[0], shape[1], 1), minval=low, maxval=high))
    return base * columns * row_scales


def draw_key_vectors(key, part):
    return multiplied_quantity(jax.random.fold_in(key, 21), (SPAN_ELEMENTS, 2, RESIDENT_ATTNS * DK)).astype(jnp.bfloat16)


def draw_value_vectors(key, part):
    return multiplied_quantity(jax.random.fold_in(key, 22), (SPAN_ELEMENTS, 2, RESIDENT_ATTNS * DV)).astype(jnp.bfloat16)


def draw_strengths(key, part):
    slow = slow_heads(key)
    fast_key, slow_key = jax.random.split(jax.random.fold_in(key, 31))
    fast = jax.random.uniform(fast_key, (2, RESIDENT_ATTNS, SPAN_ELEMENTS), minval=0.2, maxval=1.8)
    nearly = 2.0 - jax.random.uniform(slow_key, (2, RESIDENT_ATTNS, SPAN_ELEMENTS)) * (32.0 / SPAN_ELEMENTS)
    return jnp.where(slow[None, :, None], nearly, fast)


def draw_log_gate(key, part):
    slow = slow_heads(key)
    fast_key, slow_key, device_key, rough_key, placement_seed, loss_key = jax.random.split(jax.random.fold_in(key, 41), 6)
    fast_rate = jnp.exp(jax.random.uniform(fast_key, (RESIDENT_ATTNS, 1), minval=math.log(1.0 / 50.0), maxval=math.log(1.0 / 30.0)))
    slow_rate = jax.random.uniform(slow_key, (RESIDENT_ATTNS, 1), minval=0.05, maxval=0.3) * (math.log(10.0) / SPAN_ELEMENTS)
    rate = jnp.where(slow[:, None], slow_rate, fast_rate)
    block_count = SPAN_ELEMENTS // TOK_DEV
    device_factor = jnp.exp(jax.random.uniform(device_key, (RESIDENT_ATTNS, block_count, 1), minval=-math.log(2.0), maxval=math.log(2.0)))
    device_factor = jnp.broadcast_to(device_factor, (RESIDENT_ATTNS, block_count, TOK_DEV)).reshape(RESIDENT_ATTNS, SPAN_ELEMENTS)
    rough = jax.random.uniform(rough_key, (RESIDENT_ATTNS, SPAN_ELEMENTS), minval=0.5, maxval=1.5)
    spike_indices = jax.random.randint(placement_seed, (RESIDENT_ATTNS, 2), 0, SPAN_ELEMENTS)
    sequence_indices = jnp.arange(SPAN_ELEMENTS)
    agreeing_total = (sequence_indices[None, None, :] == spike_indices[:, :, None]).astype(jnp.float32)
    losses = jnp.log(jax.random.uniform(loss_key, (RESIDENT_ATTNS, 2, 1), minval=0.5, maxval=0.8))
    return -rate * device_factor * rough + jnp.sum(agreeing_total * losses, axis=1)


def block_scale(rng, dims, cuts, smallest, high):
    def one(dim, blocks):
        draws = jax.random.uniform(jax.random.fold_in(jax.random.fold_in(rng, 6), dim), (blocks,), jnp.float32, smallest / len(cuts), high / len(cuts))
        return jnp.repeat(jnp.exp(draws), dims[dim] // blocks).reshape((-1,) + (1,) * (len(dims) - dim - 1))

    loudness = one(*cuts[0])
    for cut in cuts[1:]:
        loudness = loudness * one(*cut)
    return loudness


def normal_values(own_key, shape, spread, most, cuts=(), kind=jnp.bfloat16):
    gain = block_scale(own_key, shape, cuts, -0.22, 0.18) if cuts else 1.0
    entries = jax.random.normal(own_key, shape, jnp.float32) * spread * gain
    return jnp.minimum(jnp.maximum(entries, -most), most).astype(kind)


def setup_inputs(seed: int = 0) -> dict:
    splits = jax.random.split(jax.random.key(seed), 8)
    return {
        "queries": normal_values(splits[0], (SPAN_ELEMENTS, RESIDENT_ATTNS * DK), 1.0, 6.0, ((0, 64), (1, 8))),
        "key_vectors": draw_key_vectors(jax.random.fold_in(splits[7], 71), 0),
        "value_vectors": draw_value_vectors(jax.random.fold_in(splits[7], 71), 0),
        "strengths": draw_strengths(jax.random.fold_in(splits[7], 71), 0),
        "log_gate": draw_log_gate(jax.random.fold_in(splits[7], 71), 0),
        "out_gain": jnp.clip(1.0 + 0.18 * jax.random.normal(splits[5], (RESIDENT_ATTNS * DV,), jnp.float32), 0.1, 1.9),
        "out_weight": normal_values(splits[6], (RESIDENT_ATTNS * DV, D), (RESIDENT_ATTNS * DV) ** -0.5, 0.125, ((0, 8),)),
    }


highest = lax.Precision.HIGHEST

def reference(queries, key_vectors, value_vectors, strengths, log_gate, out_gain, out_weight):
    tokens = queries.shape[0]
    query_rows = queries.astype(jnp.float32).reshape(tokens, RESIDENT_ATTNS, DK)
    key_rows = key_vectors.astype(jnp.float32).reshape(tokens, 2, RESIDENT_ATTNS, DK)
    key_rows = key_rows / jnp.sqrt(lax.optimization_barrier(jnp.sum(key_rows * key_rows, axis=-1, keepdims=True)) + 1e-06)
    value_rows = value_vectors.astype(jnp.float32).reshape(tokens, 2, RESIDENT_ATTNS, DV)
    strength_rows = jnp.transpose(strengths, (2, 0, 1))
    gate_rows = jnp.transpose(log_gate)

    def advance(state_now, step_items):
        query_one, key_pair, value_pair, strength_pair, gate_one = step_items
        state_now = state_now * jnp.exp(gate_one)[:, None, None]
        for reflect in range(2):
            key_one = key_pair[reflect]
            read_back = jnp.einsum('hde,hd->he', state_now, key_one, precision=highest)
            change = (value_pair[reflect] - read_back)[:, None, :]
            state_now = state_now + strength_pair[reflect][:, None, None] * key_one[:, :, None] * change
        return (state_now, jnp.einsum('hde,hd->he', state_now, query_one, precision=highest))
    start_state = jnp.zeros((RESIDENT_ATTNS, DK, DV), jnp.float32)
    _, outputs = lax.scan(advance, start_state, (query_rows, key_rows, value_rows, strength_rows, gate_rows))
    scale_rows = jnp.sqrt(lax.optimization_barrier(jnp.mean(outputs * outputs, axis=-1, keepdims=True)) + 1e-06)
    normed = (outputs / scale_rows * out_gain.reshape(RESIDENT_ATTNS, DV)).astype(jnp.bfloat16)
    normed = normed.reshape(tokens, RESIDENT_ATTNS * DV)
    group_width = RESIDENT_ATTNS * DV // N_TP
    summed = jnp.zeros((tokens, D), jnp.float32)
    for member in range(N_TP):
        lower = member * group_width
        upper = lower + group_width
        group_term = jnp.dot(normed[:, lower:upper], out_weight[lower:upper], preferred_element_type=jnp.float32)
        summed = summed + lax.optimization_barrier(group_term.astype(jnp.bfloat16)).astype(jnp.float32)
    return summed.astype(jnp.bfloat16)
```

```python
import functools

import jax
import jax.numpy as jnp
from jax import lax
from jax.experimental import pallas as pl
from jax.experimental.pallas import tpu as pltpu
from jax.sharding import PartitionSpec as P

MESH = pl.DeviceIdType.MESH
F32 = jnp.float32
BF16 = jnp.bfloat16
W = 128


def mm(a, b):
    return jnp.dot(a, b, preferred_element_type=F32)


def mm_nt(a, b):
    return lax.dot_general(a, b, (((1,), (1,)), ((), ())), preferred_element_type=F32)


def split2(a):
    hi = a.astype(BF16)
    return hi, (a - hi.astype(F32)).astype(BF16)


def split3(a):
    hi = a.astype(BF16)
    rest = a - hi.astype(F32)
    mid = rest.astype(BF16)
    return hi, mid, (rest - mid.astype(F32)).astype(BF16)


def dot_pairs(a, b):
    both = mm(jnp.concatenate([a[0], a[1]], axis=1), jnp.concatenate([b[0], b[0]], axis=0))
    return both + mm(a[0], b[1])


def dot_pair_one(a, b):
    return mm(jnp.concatenate([a[0], a[1]], axis=1), jnp.concatenate([b, b], axis=0))


def x3(a, b):
    return dot_pairs(split2(a), split2(b))


def spread_nt(mask, rows):
    hi, mid, lo = split3(rows)
    return mm_nt(mask, hi) + mm_nt(mask, mid) + mm_nt(mask, lo)


def spread_rows(rows, mask):
    hi, mid, lo = split3(rows)
    return mm_nt(hi, mask) + mm_nt(mid, mask) + mm_nt(lo, mask)


def iota(shape, dim):
    return lax.broadcasted_iota(jnp.int32, shape, dim)


def local_maps(keys, values, beta0, beta1, gate):
    heads = len(keys)
    step = iota((2 * W, W), 0)
    token = iota((2 * W, W), 1)
    upto = (2 * token <= step).astype(F32).astype(BF16)
    first = (2 * token == step).astype(F32).astype(BF16)
    second = (2 * token + 1 == step).astype(F32).astype(BF16)
    ones = jnp.ones((W, W), BF16)
    row = iota((W, W), 0)
    col = iota((W, W), 1)
    pre = []
    low = []
    for h in range(heads):
        k = keys[h]
        k32 = k.astype(F32)
        square = split2(k32 * k32)
        inv_col = lax.rsqrt(mm(square[0], ones) + mm(square[1], ones) + 1e-06)
        inv_row = lax.rsqrt(mm_nt(ones, square[0]) + mm_nt(ones, square[1]) + 1e-06)
        g = jnp.broadcast_to(gate[h], (W, W))
        c_col = spread_nt(upto, g)
        c_row = spread_rows(g, upto)
        beta = spread_nt(first, jnp.broadcast_to(beta0[h], (W, W))) + spread_nt(
            second, jnp.broadcast_to(beta1[h], (W, W))
        )
        gram = mm_nt(k, k)
        scaled = beta * inv_col
        blocks = {}
        for a, b in ((0, 0), (1, 1), (1, 0)):
            ra, cb = slice(a * W, a * W + W), slice(b * W, b * W + W)
            diff = c_col[ra] - c_row[:, cb]
            if a == b:
                diff = jnp.where(row > col, diff, -1e30)
            blocks[a, b] = scaled[ra] * jnp.exp(diff) * inv_row[:, cb] * gram[ra, cb]
        grow = jnp.exp(c_col)
        right = jnp.concatenate(
            [scaled * grow * k32, beta * values[h].astype(F32)], axis=1
        )
        last = c_col[2 * W - 1 : 2 * W]
        tail = inv_col * jnp.exp(last - c_col)
        pre.append((blocks[1, 0], right, tail, jnp.exp(last), c_row, inv_row, g))
        low += [blocks[0, 0], blocks[1, 1]]
    eye = (row == col).astype(F32)
    inverse = [
        eye - jnp.where((row == col + 1) & (row % 2 == 1), part, 0.0) for part in low
    ]
    size = 2
    while size < W:
        mask = (row // size == col // size + 1) & ((row // size) % 2 == 1)
        pairs = [split2(t) for t in inverse]
        inner = [
            dot_pairs(split2(jnp.where(mask, part, 0.0)), pair) for part, pair in zip(low, pairs)
        ]
        inverse = [
            t - dot_pairs(pair, split2(c)) for t, pair, c in zip(inverse, pairs, inner)
        ]
        size *= 2
    out = []
    for h in range(heads):
        below, right, tail, decay, c_row, inv_row, g = pre[h]
        top = x3(inverse[2 * h], right[:W])
        bottom = x3(inverse[2 * h + 1], right[W:] - x3(below, top))
        write = jnp.concatenate([top, bottom], axis=0)
        turned = keys[h].astype(F32).T.astype(BF16)
        weighted = split2(jnp.concatenate([tail, tail], axis=1) * write)
        both = mm(turned, weighted[0]) + mm(turned, weighted[1])
        move = jnp.where(row == col, decay, 0.0) - both[:, :W]
        out.append((move, both[:, W:], write, c_row, inv_row, g))
    return out


def local_reads(query, key, made):
    _, _, write, c_row, inv_row, g = made
    row = iota((W, W), 0)
    col = iota((W, W), 1)
    upto = (col <= row).astype(F32).astype(BF16)
    c_tok = spread_nt(upto, g)
    t = iota((W, 2 * W), 0)
    m = iota((W, 2 * W), 1)
    diff = jnp.concatenate([c_tok, c_tok], axis=1) - c_row
    ratio = jnp.exp(jnp.where(m <= 2 * t + 1, diff, -1e30))
    weights = ratio * inv_row * mm_nt(query, key)
    both = x3(weights, write)
    return jnp.exp(c_tok) * query.astype(F32) - both[:, :W], both[:, W:]


def compose(later, earlier):
    move = dot_pairs(later[0], earlier[0])
    offset = dot_pairs(later[0], split2(earlier[1])) + later[1]
    return split2(move), offset


def kernel(
    n_y,
    n_tp,
    q_ref,
    k_ref,
    v_ref,
    beta_ref,
    gate_ref,
    gain_ref,
    w_ref,
    o_ref,
    w_buf,
    y_send,
    y_recv,
    l_send,
    l_recv,
    h_send,
    h_recv,
    pre_m,
    pre_n,
    state,
    s_send,
    s_recv,
    q_eff,
    o_loc,
    n_buf,
    w_ssem,
    w_rsem,
    w_lsem,
    y_ssem,
    y_rsem,
    l_ssem,
    l_rsem,
    h_ssem,
    h_rsem,
    s_ssem,
    s_rsem,
    n_ssem,
    n_rsem,
):
    ctx = lax.axis_index("ctx")
    tp = lax.axis_index("tp")
    y = lax.rem(ctx, n_y)
    z = ctx // n_y
    zl = lax.rem(z, 4)
    zg = z // 4
    core = lax.rem(tp, 2)
    wide = 512

    def at(zz, yy):
        return zz * n_y + yy

    barrier = pltpu.get_barrier_semaphore()
    peers = [(ctx, lax.rem(tp + d, n_tp)) for d in range(1, n_tp)]
    peers += [(at(z, lax.rem(y + d, n_y)), tp) for d in range(1, n_y)]
    peers += [(at(zg * 4 + lax.rem(zl + d, 4), y), tp) for d in range(1, 4)]
    peers += [(at(lax.rem(z + 4 * d, 16), y), tp) for d in range(1, 4)]
    for peer in peers:
        pl.semaphore_signal(barrier, inc=1, device_id=peer, device_id_type=MESH)

    keys = [k_ref[:, h * W : h * W + W] for h in range(2)]
    values = [v_ref[:, h * W : h * W + W] for h in range(2)]
    beta0 = [beta_ref[h : h + 1, :] for h in range(2)]
    beta1 = [beta_ref[2 + h : 3 + h, :] for h in range(2)]
    gates = [gate_ref[h : h + 1, :] for h in range(2)]

    pl.semaphore_wait(barrier, len(peers))

    def w_columns(owner):
        return w_ref.at[:, pl.ds(pl.multiple_of(owner * wide, wide), wide)]

    w_copies = []
    for d in (4, 3, 5, 2, 6, 7, 1):
        owner = lax.rem(tp + d, n_tp)
        copy = pltpu.make_async_remote_copy(
            w_columns(owner), w_buf.at[tp], w_ssem.at[d], w_rsem.at[d], (ctx, owner), MESH
        )
        copy.start()
        w_copies.append(copy)
    w_own = pltpu.make_async_copy(w_columns(tp), w_buf.at[tp], w_lsem)
    w_own.start()

    made = local_maps(keys, values, beta0, beta1, gates)

    def y_copy(j):
        owner = 2 * core + j
        return pltpu.make_async_remote_copy(
            y_send.at[j], y_recv.at[y], y_ssem.at[j], y_rsem.at[y], (at(z, owner), tp), MESH
        )

    for j in range(2):
        move = split2(made[j][0])
        offset = made[j][1].astype(BF16)

        @pl.when(y == 2 * core + j)
        def _():
            y_recv[y, 0] = move[0]
            y_recv[y, 1] = move[1]
            y_recv[y, 2] = offset

        @pl.when(y != 2 * core + j)
        def _():
            y_send[j, 0] = move[0]
            y_send[j, 1] = move[1]
            y_send[j, 2] = offset
            y_copy(j).start()

    for j in range(2):
        eff, loc = local_reads(q_ref[:, j * W : j * W + W], keys[j], made[j])
        hi, lo = split2(eff)
        q_eff[j, :, :W] = hi
        q_eff[j, :, W:] = lo
        o_loc[j] = loc

    def s_copy(target, j):
        return pltpu.make_async_remote_copy(
            s_send.at[target], s_recv.at[j], s_ssem.at[target], s_rsem.at[j],
            (at(z, target), tp), MESH,
        )

    def l_copy(d):
        other = lax.rem(zl + d, 4)
        return pltpu.make_async_remote_copy(
            l_send, l_recv.at[zl], l_ssem.at[d], l_rsem.at[zl], (at(zg * 4 + other, y), tp), MESH
        )

    def h_copy(d):
        return pltpu.make_async_remote_copy(
            h_send, h_recv.at[zg], h_ssem.at[d], h_rsem.at[zg],
            (at(lax.rem(z + 4 * d, 16), y), tp), MESH,
        )

    mine = lax.rem(y, 2)

    @pl.when(y // 2 == core)
    def _():
        for s in range(n_y):

            @pl.when(s != y)
            def _():
                pltpu.make_async_remote_copy(
                    y_recv.at[s], y_recv.at[s], y_ssem.at[0], y_rsem.at[s],
                    (at(z, s), tp), MESH,
                ).wait_recv()

        part = [
            ((y_recv[s, 0], y_recv[s, 1]), y_recv[s, 2].astype(F32)) for s in range(n_y)
        ]
        first_two = compose(part[1], part[0])
        last_two = compose(part[3], part[2])
        whole = compose(last_two, first_two)
        l_send[0] = whole[0][0]
        l_send[1] = whole[1].astype(BF16)
        for d in (3, 1, 2):
            l_copy(d).start()
        l_recv[zl, 0] = whole[0][0]
        l_recv[zl, 1] = whole[1].astype(BF16)
        three = compose(part[2], first_two)
        row = iota((W, W), 0)
        col = iota((W, W), 1)
        eye = (row == col).astype(F32)
        for d in range(1, 4):
            src = lax.rem(zl + d, 4)
            pltpu.make_async_remote_copy(
                l_recv.at[src], l_recv.at[src], l_ssem.at[d], l_rsem.at[src],
                (at(zg * 4 + src, y), tp), MESH,
            ).wait_recv()
        none = jnp.zeros((W, W), BF16)
        grp = [((l_recv[s, 0], none), l_recv[s, 1].astype(F32)) for s in range(4)]
        low_two = compose(grp[1], grp[0])
        high_two = compose(grp[3], grp[2])
        total = compose(high_two, low_two)
        h_send[0] = total[0][0]
        h_send[1] = total[1].astype(BF16)
        for d in (2, 3, 1):

            @pl.when(zg + d < 4)
            def _():
                h_copy(d).start()

        low_three = compose(grp[2], low_two)
        entry_m = jnp.where(
            zl == 0,
            eye,
            jnp.where(
                zl == 1,
                grp[0][0][0].astype(F32),
                jnp.where(
                    zl == 2,
                    low_two[0][0].astype(F32) + low_two[0][1].astype(F32),
                    low_three[0][0].astype(F32) + low_three[0][1].astype(F32),
                ),
            ),
        )
        entry_n = jnp.where(
            zl == 0,
            0.0,
            jnp.where(zl == 1, grp[0][1], jnp.where(zl == 2, low_two[1], low_three[1])),
        )
        entry = (split2(entry_m), entry_n)
        starts = [entry] + [compose(p, entry) for p in (part[0], first_two, three)]
        for s in range(n_y):
            pre_m[s, :, :W] = starts[s][0][0]
            pre_m[s, :, W:] = starts[s][0][1]
            pre_n[s] = starts[s][1]
        state[...] = jnp.zeros((W, W), F32)
        for s in range(3):

            @pl.when(s < zg)
            def _():
                pltpu.make_async_remote_copy(
                    h_recv.at[s], h_recv.at[s], h_ssem.at[0], h_rsem.at[s],
                    (at(z, y), tp), MESH,
                ).wait_recv()
                if s == 0:
                    state[...] = h_recv[s, 1].astype(F32)
                else:
                    now = split2(state[...])
                    state[...] = mm(
                        jnp.concatenate([h_recv[s, 0], h_recv[s, 0]], axis=1),
                        jnp.concatenate([now[0], now[1]], axis=0),
                    ) + h_recv[s, 1].astype(F32)

        now = split2(state[...])
        for s in range(n_y):
            both = pre_m[s]
            moved = mm(both, jnp.concatenate([now[0], now[0]], axis=0)) + mm(both[:, :W], now[1])
            s_send[s] = (moved + pre_n[s]).astype(BF16)
        for d in (2, 1, 3):
            s_copy(lax.rem(y + d, n_y), mine).start()
        s_recv[mine] = s_send[y]

    for j in range(2):

        @pl.when(y != 2 * core + j)
        def _():
            pltpu.make_async_remote_copy(
                s_recv.at[j], s_recv.at[j], s_ssem.at[0], s_rsem.at[j],
                (at(z, 2 * core + j), tp), MESH,
            ).wait_recv()

        entering = s_recv[j]
        out = mm(q_eff[j], jnp.concatenate([entering, entering], axis=0)) + o_loc[j]
        scale = lax.rsqrt(jnp.mean(out * out, axis=1, keepdims=True) + 1e-06)
        gain = gain_ref[:, j * W : j * W + W]
        n_buf[tp, :, j * W : j * W + W] = (out * scale * gain).astype(BF16)

    n_copies = []
    for d in (4, 3, 5, 2, 6, 7, 1):
        other = lax.rem(tp + d, n_tp)
        copy = pltpu.make_async_remote_copy(
            n_buf.at[tp], n_buf.at[tp], n_ssem.at[d], n_rsem.at[d], (ctx, other), MESH
        )
        copy.start()
        n_copies.append(copy)
    w_own.wait()
    total = mm(n_buf[tp], w_buf[tp])
    for d in (1, 7, 2, 6, 3, 5, 4):
        src = lax.rem(tp + n_tp - d, n_tp)
        for buf, ssem, rsem in ((w_buf, w_ssem, w_rsem), (n_buf, n_ssem, n_rsem)):
            pltpu.make_async_remote_copy(
                buf.at[src], buf.at[src], ssem.at[d], rsem.at[d], (ctx, src), MESH
            ).wait_recv()
        total = total + mm(n_buf[src], w_buf[src])
    o_ref[...] = total.astype(BF16)

    for copy in w_copies + n_copies:
        copy.wait_send()
    for j in range(2):

        @pl.when(y != 2 * core + j)
        def _():
            y_copy(j).wait_send()

    @pl.when(y // 2 == core)
    def _():
        for d in range(1, 4):
            l_copy(d).wait_send()

            @pl.when(zg + d < 4)
            def _():
                h_copy(d).wait_send()

            s_copy(lax.rem(y + d, n_y), mine).wait_send()


def local(queries, key_vectors, value_vectors, strengths, log_gate, out_gain, out_weight):
    tokens = queries.shape[0]
    n_tp = 8
    n_y = 4
    width = out_weight.shape[1] // n_tp
    vmem = pl.BlockSpec(memory_space=pltpu.VMEM)
    dma = pltpu.SemaphoreType.DMA
    return pl.pallas_call(
        functools.partial(kernel, n_y, n_tp),
        out_shape=jax.ShapeDtypeStruct((tokens, width), BF16),
        in_specs=[vmem] * 6 + [pl.BlockSpec(memory_space=pl.ANY)],
        out_specs=vmem,
        scratch_shapes=[
            pltpu.VMEM((n_tp, 2 * W, width), BF16),
            pltpu.VMEM((2, 3, W, W), BF16),
            pltpu.VMEM((n_y, 3, W, W), BF16),
            pltpu.VMEM((2, W, W), BF16),
            pltpu.VMEM((4, 2, W, W), BF16),
            pltpu.VMEM((2, W, W), BF16),
            pltpu.VMEM((4, 2, W, W), BF16),
            pltpu.VMEM((n_y, W, 2 * W), BF16),
            pltpu.VMEM((n_y, W, W), F32),
            pltpu.VMEM((W, W), F32),
            pltpu.VMEM((n_y, W, W), BF16),
            pltpu.VMEM((2, W, W), BF16),
            pltpu.VMEM((2, W, 2 * W), BF16),
            pltpu.VMEM((2, W, W), F32),
            pltpu.VMEM((n_tp, W, 2 * W), BF16),
            dma((n_tp,)),
            dma((n_tp,)),
            dma,
            dma((2,)),
            dma((n_y,)),
            dma((4,)),
            dma((4,)),
            dma((4,)),
            dma((4,)),
            dma((n_y,)),
            dma((2,)),
            dma((n_tp,)),
            dma((n_tp,)),
        ],
        compiler_params=pltpu.CompilerParams(collective_id=0, has_side_effects=True),
    )(
        queries,
        key_vectors.reshape(2 * tokens, -1),
        value_vectors.reshape(2 * tokens, -1),
        strengths.reshape(4, tokens),
        log_gate,
        out_gain.reshape(1, -1),
        out_weight,
    )


def solution(mesh):
    placed = (
        P("ctx", "tp"),
        P("ctx", None, "tp"),
        P("ctx", None, "tp"),
        P(None, "tp", "ctx"),
        P("tp", "ctx"),
        P("tp"),
        P("tp", None),
    )
    return jax.shard_map(
        local, mesh=mesh, in_specs=placed, out_specs=P("ctx", "tp"), check_vma=False
    )
```

```python
import functools

import jax
import jax.numpy as jnp
from jax import lax
from jax.experimental import pallas as pl
from jax.experimental.pallas import tpu as pltpu
from jax.sharding import PartitionSpec as P

MESH = pl.DeviceIdType.MESH
F32 = jnp.float32
BF16 = jnp.bfloat16
W = 128


def mm(a, b):
    return jnp.dot(a, b, preferred_element_type=F32)


def mm_nt(a, b):
    return lax.dot_general(a, b, (((1,), (1,)), ((), ())), preferred_element_type=F32)


def split2(a):
    hi = a.astype(BF16)
    return hi, (a - hi.astype(F32)).astype(BF16)


def split3(a):
    hi = a.astype(BF16)
    rest = a - hi.astype(F32)
    mid = rest.astype(BF16)
    return hi, mid, (rest - mid.astype(F32)).astype(BF16)


def left3(pair):
    return jnp.concatenate([pair[0], pair[1], pair[0]], axis=1)


def right3(pair):
    return jnp.concatenate([pair[0], pair[0], pair[1]], axis=0)


def dot_pairs(a, b):
    return mm(left3(a), right3(b))


def dot_pair_one(a, b):
    return mm(jnp.concatenate([a[0], a[1]], axis=1), jnp.concatenate([b, b], axis=0))


def x3(a, b):
    return dot_pairs(split2(a), split2(b))


def iota(shape, dim):
    return lax.broadcasted_iota(jnp.int32, shape, dim)


def bits(mask):
    return mask.astype(F32).astype(BF16)


def by_rows(block, rows):
    n = block.shape[0]
    return block.reshape(n // 8, 8, W), jnp.broadcast_to(rows[None], (n // 8, 8, W))


def times_rows(block, rows):
    a, b = by_rows(block, rows)
    return (a * b).reshape(block.shape)


def minus_rows(block, rows):
    a, b = by_rows(block, rows)
    return (a - b).reshape(block.shape)


def make_masks():
    step = iota((2 * W, W), 0)
    token = iota((2 * W, W), 1)
    row = iota((W, W), 0)
    col = iota((W, W), 1)
    upto = bits(2 * token <= step)
    first = bits(2 * token == step)
    second = bits(2 * token + 1 == step)
    levels = []
    size = 1
    while size < W:
        levels.append(bits((row // size == col // size + 1) & ((row // size) % 2 == 1)))
        size *= 2
    return (
        jnp.concatenate([upto] * 3, axis=1),
        jnp.concatenate([first] * 3 + [second] * 3, axis=1),
        levels,
    )


def local_maps(masks, keys, values, beta0, beta1, gate):
    heads = len(keys)
    upto3, pick, levels = masks
    row = iota((W, W), 0)
    col = iota((W, W), 1)
    eye = (row == col).astype(F32)
    pre = []
    low = []
    for h in range(heads):
        k = keys[h]
        k32 = k.astype(F32)
        gram = mm_nt(k, k)
        inv_col = lax.rsqrt(jnp.sum(k32 * k32, axis=1, keepdims=True) + 1e-06)
        inv_row = []
        for a in range(2):
            part = jnp.where(row == col, gram[a * W : a * W + W, a * W : a * W + W], 0.0)
            total = jnp.sum(part.reshape(W // 8, 8, W), axis=0)
            total = jnp.broadcast_to(jnp.sum(total, axis=0, keepdims=True), (8, W))
            inv_row.append(lax.rsqrt(total + 1e-06))
        g3 = jnp.concatenate(split3(jnp.broadcast_to(gate[h], (W, W))), axis=1)
        b3 = jnp.concatenate(
            split3(jnp.broadcast_to(beta0[h], (W, W))) + split3(jnp.broadcast_to(beta1[h], (W, W))),
            axis=1,
        )
        c_col = mm_nt(upto3, g3)
        c_row = mm_nt(g3[:8], upto3)
        beta = mm_nt(pick, b3)
        beta_row = mm_nt(b3[:8], pick)
        grow_row = jnp.exp(c_row)
        scaled = beta * inv_col
        blocks = {}
        for a, b in ((0, 0), (1, 1), (1, 0)):
            ra, cb = slice(a * W, a * W + W), slice(b * W, b * W + W)
            diff = minus_rows(c_col[ra], c_row[:, cb])
            if a == b:
                diff = jnp.where(row > col, diff, -1e30)
            block = scaled[ra] * jnp.exp(diff) * times_rows(gram[ra, cb], inv_row[b])
            blocks[a, b] = split2(block)
        last = c_col[2 * W - 1 : 2 * W]
        tail = inv_col * jnp.exp(last - c_col)
        pre.append((blocks[1, 0], beta_row, grow_row, inv_row, tail, jnp.exp(last), c_row, g3))
        low += [blocks[0, 0], blocks[1, 1]]
    inverse = [
        eye - (part[0] * levels[0]).astype(F32) - (part[1] * levels[0]).astype(F32) for part in low
    ]
    for mask in levels[1:]:
        pairs = [split2(t) for t in inverse]
        inner = [
            dot_pairs((part[0] * mask, part[1] * mask), pair) for part, pair in zip(low, pairs)
        ]
        inverse = [t - dot_pairs(pair, split2(c)) for t, pair, c in zip(inverse, pairs, inner)]
    out = []
    pairs = [split2(t) for t in inverse]
    inner = [dot_pairs(pre[h][0], pairs[2 * h]) for h in range(heads)]
    below = [dot_pairs(pairs[2 * h + 1], split2(inner[h])) for h in range(heads)]
    for h in range(heads):
        _, beta_row, grow_row, inv_row, tail, decay, c_row, g3 = pre[h]
        top = []
        bottom = []
        for which, data in ((0, keys[h]), (1, values[h])):
            scale = [beta_row[:, a * W : a * W + W] for a in range(2)]
            if which == 0:
                scale = [
                    scale[a] * grow_row[:, a * W : a * W + W] * inv_row[a] for a in range(2)
                ]
            t00 = split2(times_rows(inverse[2 * h], scale[0]))
            t10 = split2(times_rows(below[h], -scale[0]))
            t11 = split2(times_rows(inverse[2 * h + 1], scale[1]))
            d0, d1 = data[:W], data[W:]
            top.append(
                mm(jnp.concatenate(t00, axis=1), jnp.concatenate([d0, d0], axis=0))
            )
            bottom.append(
                mm(
                    jnp.concatenate([t10[0], t11[0], t10[1], t11[1]], axis=1),
                    jnp.concatenate([d0, d1, d0, d1], axis=0),
                )
            )
        write = jnp.concatenate(
            [jnp.concatenate(top, axis=1), jnp.concatenate(bottom, axis=1)], axis=0
        )
        turned = keys[h].astype(F32).T.astype(BF16)
        weighted = split2(jnp.concatenate([tail, tail], axis=1) * write)
        both = mm(jnp.concatenate([turned, turned], axis=1), jnp.concatenate(weighted, axis=0))
        move = jnp.where(row == col, decay, 0.0) - both[:, :W]
        out.append((move, both[:, W:], write, c_row, inv_row, g3))
    return out


def local_reads(query, key, made):
    _, _, write, c_row, inv_row, g3 = made
    row = iota((W, W), 0)
    col = iota((W, W), 1)
    upto = bits(col <= row)
    c_tok = mm_nt(jnp.concatenate([upto] * 3, axis=1), g3)
    seen = mm_nt(query, key)
    weights = []
    for a in range(2):
        cols = slice(a * W, a * W + W)
        diff = minus_rows(c_tok, c_row[:, cols])
        ratio = jnp.exp(jnp.where(col + a * W <= 2 * row + 1, diff, -1e30))
        weights.append(ratio * times_rows(seen[:, cols], inv_row[a]))
    both = x3(jnp.concatenate(weights, axis=1), write)
    return jnp.exp(c_tok) * query.astype(F32) - both[:, :W], both[:, W:]


def compose(later, earlier):
    move = dot_pairs(later[0], earlier[0])
    offset = dot_pairs(later[0], split2(earlier[1])) + later[1]
    return split2(move), offset


def kernel(
    n_y,
    n_tp,
    q_ref,
    k_ref,
    v_ref,
    beta_ref,
    gate_ref,
    gain_ref,
    w_ref,
    o_ref,
    k_buf,
    v_buf,
    w_buf,
    y_send,
    y_recv,
    l_send,
    l_recv,
    h_send,
    h_recv,
    pre_m,
    pre_n,
    state,
    s_send,
    s_recv,
    q_eff,
    o_loc,
    n_buf,
    w_ssem,
    w_rsem,
    w_lsem,
    y_ssem,
    y_rsem,
    l_ssem,
    l_rsem,
    h_ssem,
    h_rsem,
    s_ssem,
    s_rsem,
    n_ssem,
    n_rsem,
    f_ssem,
    i_sem,
    ready,
):
    ctx = lax.axis_index("ctx")
    tp = lax.axis_index("tp")
    y = lax.rem(ctx, n_y)
    z = ctx // n_y
    zl = lax.rem(z, 4)
    zg = z // 4
    core = lax.rem(tp, 2)
    wide = 512

    def at(zz, yy):
        return zz * n_y + yy

    loads = []
    for i, (ref, buf) in enumerate(((k_ref, k_buf), (v_ref, v_buf))):
        for h in range(2):
            copy = pltpu.make_async_copy(
                ref.reshape(2 * W, 2 * W).at[:, pl.ds(h * W, W)], buf.at[h], i_sem.at[2 * i + h]
            )
            copy.start()
            loads.append(copy)

    barrier = pltpu.get_barrier_semaphore()
    near = [(ctx, lax.rem(tp + d, n_tp)) for d in range(1, n_tp)]
    near += [(at(z, lax.rem(y + d, n_y)), tp) for d in range(1, n_y)]
    near += [(at(zg * 4 + lax.rem(zl + d, 4), y), tp) for d in range(1, 4)]
    for peer in near:
        pl.semaphore_signal(barrier, inc=1, device_id=peer, device_id_type=MESH)
    for d in range(1, 4):

        @pl.when(zg + d < 4)
        def _():
            pl.semaphore_signal(
                barrier, inc=1, device_id=(at(lax.rem(z + 4 * d, 16), y), tp), device_id_type=MESH
            )

    masks = make_masks()
    for copy in loads:
        copy.wait()
    keys = [k_buf[h] for h in range(2)]
    values = [v_buf[h] for h in range(2)]
    beta0 = [beta_ref[h : h + 1, :] for h in range(2)]
    beta1 = [beta_ref[2 + h : 3 + h, :] for h in range(2)]
    gates = [gate_ref[h : h + 1, :] for h in range(2)]

    pl.semaphore_wait(barrier, len(near) + zg)
    for d in range(1, 4):

        @pl.when(zg - d >= 0)
        def _():
            pl.semaphore_signal(
                ready, inc=1, device_id=(at(lax.rem(z + 16 - 4 * d, 16), y), tp),
                device_id_type=MESH,
            )

    def w_columns(owner):
        return w_ref.at[:, pl.ds(pl.multiple_of(owner * wide, wide), wide)]

    w_copies = []
    for d in (4, 3, 5, 2, 6, 7, 1):
        owner = lax.rem(tp + d, n_tp)
        copy = pltpu.make_async_remote_copy(
            w_columns(owner), w_buf.at[tp], w_ssem.at[d], w_rsem.at[tp], (ctx, owner), MESH
        )
        copy.start()
        w_copies.append(copy)
    w_own = pltpu.make_async_copy(w_columns(tp), w_buf.at[tp], w_lsem)
    w_own.start()

    made = local_maps(masks, keys, values, beta0, beta1, gates)

    def y_copy(j):
        owner = 2 * core + j
        return pltpu.make_async_remote_copy(
            y_send.at[j], y_recv.at[y], y_ssem.at[j], y_rsem.at[y], (at(z, owner), tp), MESH
        )

    for j in range(2):
        move = split2(made[j][0])
        offset = made[j][1].astype(BF16)

        @pl.when(y == 2 * core + j)
        def _():
            y_recv[y, 0] = move[0]
            y_recv[y, 1] = move[1]
            y_recv[y, 2] = offset

        @pl.when(y != 2 * core + j)
        def _():
            y_send[j, 0] = move[0]
            y_send[j, 1] = move[1]
            y_send[j, 2] = offset
            y_copy(j).start()

    for j in range(2):
        eff, loc = local_reads(q_ref[:, j * W : j * W + W], keys[j], made[j])
        hi, lo = split2(eff)
        q_eff[j, :, :W] = hi
        q_eff[j, :, W:] = lo
        o_loc[j] = loc

    def s_copy(target, j):
        return pltpu.make_async_remote_copy(
            s_send.at[target], s_recv.at[j], s_ssem.at[target], s_rsem.at[j],
            (at(z, target), tp), MESH,
        )

    def l_copy(d):
        other = lax.rem(zl + d, 4)
        return pltpu.make_async_remote_copy(
            l_send, l_recv.at[zl], l_ssem.at[d], l_rsem.at[zl], (at(zg * 4 + other, y), tp), MESH
        )

    def h_copy(d):
        return pltpu.make_async_remote_copy(
            h_send, h_recv.at[zg], h_ssem.at[d], h_rsem.at[zg],
            (at(lax.rem(z + 4 * d, 16), y), tp), MESH,
        )

    mine = lax.rem(y, 2)

    def ready_wait():
        @pl.when(zg < 3)
        def _():
            pl.semaphore_wait(ready, 3 - zg)

    @pl.when(y // 2 != core)
    def _():
        ready_wait()

    @pl.when(y // 2 == core)
    def _():
        for s in range(n_y):

            @pl.when(s != y)
            def _():
                pltpu.make_async_remote_copy(
                    y_recv.at[s], y_recv.at[s], y_ssem.at[0], y_rsem.at[s],
                    (at(z, s), tp), MESH,
                ).wait_recv()

        part = [
            ((y_recv[s, 0], y_recv[s, 1]), y_recv[s, 2].astype(F32)) for s in range(n_y)
        ]
        first_two = compose(part[1], part[0])
        last_two = compose(part[3], part[2])
        whole = compose(last_two, first_two)
        l_send[0] = whole[0][0]
        l_send[1] = whole[1].astype(BF16)
        for d in (3, 1, 2):
            l_copy(d).start()
        l_recv[zl, 0] = whole[0][0]
        l_recv[zl, 1] = whole[1].astype(BF16)
        three = compose(part[2], first_two)
        row = iota((W, W), 0)
        col = iota((W, W), 1)
        eye = (row == col).astype(F32)
        for d in range(1, 4):
            src = lax.rem(zl + d, 4)
            pltpu.make_async_remote_copy(
                l_recv.at[src], l_recv.at[src], l_ssem.at[d], l_rsem.at[src],
                (at(zg * 4 + src, y), tp), MESH,
            ).wait_recv()
        none = jnp.zeros((W, W), BF16)
        grp = [((l_recv[s, 0], none), l_recv[s, 1].astype(F32)) for s in range(4)]
        low_two = compose(grp[1], grp[0])
        high_two = compose(grp[3], grp[2])
        total = compose(high_two, low_two)
        h_send[0] = total[0][0]
        h_send[1] = total[1].astype(BF16)
        ready_wait()
        for d in (2, 3, 1):

            @pl.when(zg + d < 4)
            def _():
                h_copy(d).start()

        low_three = compose(grp[2], low_two)
        entry_m = jnp.where(
            zl == 0,
            eye,
            jnp.where(
                zl == 1,
                grp[0][0][0].astype(F32),
                jnp.where(
                    zl == 2,
                    low_two[0][0].astype(F32) + low_two[0][1].astype(F32),
                    low_three[0][0].astype(F32) + low_three[0][1].astype(F32),
                ),
            ),
        )
        entry_n = jnp.where(
            zl == 0,
            0.0,
            jnp.where(zl == 1, grp[0][1], jnp.where(zl == 2, low_two[1], low_three[1])),
        )
        entry = (split2(entry_m), entry_n)
        starts = [entry] + [compose(p, entry) for p in (part[0], first_two, three)]
        for s in range(n_y):
            pre_m[s, :, :W] = starts[s][0][0]
            pre_m[s, :, W:] = starts[s][0][1]
            pre_n[s] = starts[s][1]
        state[...] = jnp.zeros((W, W), F32)
        for s in range(3):

            @pl.when(s < zg)
            def _():
                pltpu.make_async_remote_copy(
                    h_recv.at[s], h_recv.at[s], h_ssem.at[0], h_rsem.at[s],
                    (at(z, y), tp), MESH,
                ).wait_recv()
                if s == 0:
                    state[...] = h_recv[s, 1].astype(F32)
                else:
                    now = split2(state[...])
                    state[...] = mm(
                        jnp.concatenate([h_recv[s, 0], h_recv[s, 0]], axis=1),
                        jnp.concatenate([now[0], now[1]], axis=0),
                    ) + h_recv[s, 1].astype(F32)

        now = split2(state[...])
        for s in range(n_y):
            both = pre_m[s]
            moved = mm(both, jnp.concatenate([now[0], now[0]], axis=0)) + mm(both[:, :W], now[1])
            s_send[s] = (moved + pre_n[s]).astype(BF16)
        for d in (2, 1, 3):
            s_copy(lax.rem(y + d, n_y), mine).start()
        s_recv[mine] = s_send[y]

    for j in range(2):

        @pl.when(y != 2 * core + j)
        def _():
            pltpu.make_async_remote_copy(
                s_recv.at[j], s_recv.at[j], s_ssem.at[0], s_rsem.at[j],
                (at(z, 2 * core + j), tp), MESH,
            ).wait_recv()

        entering = s_recv[j]
        out = mm(q_eff[j], jnp.concatenate([entering, entering], axis=0)) + o_loc[j]
        scale = lax.rsqrt(jnp.mean(out * out, axis=1, keepdims=True) + 1e-06)
        gain = gain_ref[:, j * W : j * W + W]
        n_buf[tp, :, j * W : j * W + W] = (out * scale * gain).astype(BF16)

    chip = tp // 2
    partner = chip * 2 + 1 - core

    def n_copy(d):
        other = lax.rem(chip + d, 4) * 2 + core
        return pltpu.make_async_remote_copy(
            n_buf.at[tp], n_buf.at[tp], n_ssem.at[d], n_rsem.at[tp], (ctx, other), MESH
        )

    def pass_on(d):
        src = lax.rem(chip + d, 4) * 2 + core
        return pltpu.make_async_remote_copy(
            n_buf.at[src], n_buf.at[src], f_ssem.at[d], n_rsem.at[src], (ctx, partner), MESH
        )

    def arrived(src):
        pltpu.make_async_remote_copy(
            n_buf.at[src], n_buf.at[src], f_ssem.at[0], n_rsem.at[src], (ctx, partner), MESH
        ).wait_recv()

    def w_arrived(src):
        pltpu.make_async_remote_copy(
            w_buf.at[src], w_buf.at[src], w_ssem.at[0], w_rsem.at[src], (ctx, partner), MESH
        ).wait_recv()

    for d in (2, 1, 3):
        n_copy(d).start()
    pass_on(0).start()
    w_own.wait()
    total = mm(n_buf[tp], w_buf[tp])
    w_arrived(partner)
    arrived(partner)
    total = total + mm(n_buf[partner], w_buf[partner])
    for d in (1, 3, 2):
        src = lax.rem(chip + d, 4) * 2 + core
        arrived(src)
        pass_on(d).start()
        w_arrived(src)
        total = total + mm(n_buf[src], w_buf[src])
    for d in (1, 3, 2):
        src = lax.rem(chip + d, 4) * 2 + 1 - core
        w_arrived(src)
        arrived(src)
        total = total + mm(n_buf[src], w_buf[src])
    o_ref[...] = total.astype(BF16)

    for copy in w_copies:
        copy.wait_send()
    for d in range(4):
        pass_on(d).wait_send()
    for d in range(1, 4):
        n_copy(d).wait_send()
    for j in range(2):

        @pl.when(y != 2 * core + j)
        def _():
            y_copy(j).wait_send()

    @pl.when(y // 2 == core)
    def _():
        for d in range(1, 4):
            l_copy(d).wait_send()

            @pl.when(zg + d < 4)
            def _():
                h_copy(d).wait_send()

            s_copy(lax.rem(y + d, n_y), mine).wait_send()


def local(queries, key_vectors, value_vectors, strengths, log_gate, out_gain, out_weight):
    tokens = queries.shape[0]
    n_tp = 8
    n_y = 4
    width = out_weight.shape[1] // n_tp
    vmem = pl.BlockSpec(memory_space=pltpu.VMEM)
    hbm = pl.BlockSpec(memory_space=pl.ANY)
    dma = pltpu.SemaphoreType.DMA
    return pl.pallas_call(
        functools.partial(kernel, n_y, n_tp),
        out_shape=jax.ShapeDtypeStruct((tokens, width), BF16),
        in_specs=[vmem, hbm, hbm, vmem, vmem, vmem, hbm],
        out_specs=vmem,
        scratch_shapes=[
            pltpu.VMEM((2, 2 * W, W), BF16),
            pltpu.VMEM((2, 2 * W, W), BF16),
            pltpu.VMEM((n_tp, 2 * W, width), BF16),
            pltpu.VMEM((2, 3, W, W), BF16),
            pltpu.VMEM((n_y, 3, W, W), BF16),
            pltpu.VMEM((2, W, W), BF16),
            pltpu.VMEM((4, 2, W, W), BF16),
            pltpu.VMEM((2, W, W), BF16),
            pltpu.VMEM((4, 2, W, W), BF16),
            pltpu.VMEM((n_y, W, 2 * W), BF16),
            pltpu.VMEM((n_y, W, W), F32),
            pltpu.VMEM((W, W), F32),
            pltpu.VMEM((n_y, W, W), BF16),
            pltpu.VMEM((2, W, W), BF16),
            pltpu.VMEM((2, W, 2 * W), BF16),
            pltpu.VMEM((2, W, W), F32),
            pltpu.VMEM((n_tp, W, 2 * W), BF16),
            dma((n_tp,)),
            dma((n_tp,)),
            dma,
            dma((2,)),
            dma((n_y,)),
            dma((4,)),
            dma((4,)),
            dma((4,)),
            dma((4,)),
            dma((n_y,)),
            dma((2,)),
            dma((4,)),
            dma((n_tp,)),
            dma((4,)),
            dma((4,)),
            pltpu.SemaphoreType.REGULAR,
        ],
        compiler_params=pltpu.CompilerParams(collective_id=0, has_side_effects=True),
    )(
        queries,
        key_vectors,
        value_vectors,
        strengths.reshape(4, tokens),
        log_gate,
        out_gain.reshape(1, -1),
        out_weight,
    )


def solution(mesh):
    placed = (
        P("ctx", "tp"),
        P("ctx", None, "tp"),
        P("ctx", None, "tp"),
        P(None, "tp", "ctx"),
        P("tp", "ctx"),
        P("tp"),
        P("tp", None),
    )
    return jax.shard_map(
        local, mesh=mesh, in_specs=placed, out_specs=P("ctx", "tp"), check_vma=False
    )
```

```python
import functools

import jax
import jax.numpy as jnp
from jax import lax
from jax.experimental import pallas as pl
from jax.experimental.pallas import tpu as pltpu
from jax.sharding import PartitionSpec as P

MESH = pl.DeviceIdType.MESH
F32 = jnp.float32
BF16 = jnp.bfloat16
W = 128


def mm(a, b):
    return jnp.dot(a, b, preferred_element_type=F32)


def mm_nt(a, b):
    return lax.dot_general(a, b, (((1,), (1,)), ((), ())), preferred_element_type=F32)


def split2(a):
    hi = a.astype(BF16)
    return hi, (a - hi.astype(F32)).astype(BF16)


def split3(a):
    hi = a.astype(BF16)
    rest = a - hi.astype(F32)
    mid = rest.astype(BF16)
    return hi, mid, (rest - mid.astype(F32)).astype(BF16)


def left3(pair):
    return jnp.concatenate([pair[0], pair[1], pair[0]], axis=1)


def right3(pair):
    return jnp.concatenate([pair[0], pair[0], pair[1]], axis=0)


def dot_pairs(a, b):
    return mm(left3(a), right3(b))


def dot_pair_one(a, b):
    return mm(jnp.concatenate([a[0], a[1]], axis=1), jnp.concatenate([b, b], axis=0))


def x3(a, b):
    return dot_pairs(split2(a), split2(b))


def iota(shape, dim):
    return lax.broadcasted_iota(jnp.int32, shape, dim)


def bits(mask):
    return mask.astype(F32).astype(BF16)


def by_rows(block, rows):
    n = block.shape[0]
    return block.reshape(n // 8, 8, W), jnp.broadcast_to(rows[None], (n // 8, 8, W))


def times_rows(block, rows):
    a, b = by_rows(block, rows)
    return (a * b).reshape(block.shape)


def minus_rows(block, rows):
    a, b = by_rows(block, rows)
    return (a - b).reshape(block.shape)


def make_masks():
    step = iota((2 * W, W), 0)
    token = iota((2 * W, W), 1)
    row = iota((W, W), 0)
    col = iota((W, W), 1)
    upto = bits(2 * token <= step)
    first = bits(2 * token == step)
    second = bits(2 * token + 1 == step)
    levels = []
    size = 1
    while size < W:
        levels.append(bits((row // size == col // size + 1) & ((row // size) % 2 == 1)))
        size *= 2
    return (
        jnp.concatenate([upto] * 3, axis=1),
        jnp.concatenate([first] * 3 + [second] * 3, axis=1),
        levels,
    )


def local_maps(masks, keys, values, beta0, beta1, gate):
    heads = len(keys)
    upto3, pick, levels = masks
    row = iota((W, W), 0)
    col = iota((W, W), 1)
    eye = (row == col).astype(F32)
    pre = []
    low = []
    for h in range(heads):
        k = keys[h]
        k32 = k.astype(F32)
        gram = mm_nt(k, k)
        inv_col = lax.rsqrt(jnp.sum(k32 * k32, axis=1, keepdims=True) + 1e-06)
        inv_row = []
        for a in range(2):
            part = jnp.where(row == col, gram[a * W : a * W + W, a * W : a * W + W], 0.0)
            total = jnp.sum(part.reshape(W // 8, 8, W), axis=0)
            total = jnp.broadcast_to(jnp.sum(total, axis=0, keepdims=True), (8, W))
            inv_row.append(lax.rsqrt(total + 1e-06))
        g3 = jnp.concatenate(split3(jnp.broadcast_to(gate[h], (W, W))), axis=1)
        b3 = jnp.concatenate(
            split3(jnp.broadcast_to(beta0[h], (W, W))) + split3(jnp.broadcast_to(beta1[h], (W, W))),
            axis=1,
        )
        c_col = mm_nt(upto3, g3)
        c_row = mm_nt(g3[:8], upto3)
        beta = mm_nt(pick, b3)
        beta_row = mm_nt(b3[:8], pick)
        grow_row = jnp.exp(c_row)
        scaled = beta * inv_col
        blocks = {}
        for a, b in ((0, 0), (1, 1), (1, 0)):
            ra, cb = slice(a * W, a * W + W), slice(b * W, b * W + W)
            diff = minus_rows(c_col[ra], c_row[:, cb])
            if a == b:
                diff = jnp.where(row > col, diff, -1e30)
            block = scaled[ra] * jnp.exp(diff) * times_rows(gram[ra, cb], inv_row[b])
            blocks[a, b] = split2(block)
        last = c_col[2 * W - 1 : 2 * W]
        tail = inv_col * jnp.exp(last - c_col)
        pre.append((blocks[1, 0], beta_row, grow_row, inv_row, tail, jnp.exp(last), c_row, g3))
        low += [blocks[0, 0], blocks[1, 1]]
    inverse = [
        eye - (part[0] * levels[0]).astype(F32) - (part[1] * levels[0]).astype(F32) for part in low
    ]
    for mask in levels[1:]:
        pairs = [split2(t) for t in inverse]
        inner = [
            dot_pairs((part[0] * mask, part[1] * mask), pair) for part, pair in zip(low, pairs)
        ]
        inverse = [t - dot_pairs(pair, split2(c)) for t, pair, c in zip(inverse, pairs, inner)]
    out = []
    pairs = [split2(t) for t in inverse]
    inner = [dot_pairs(pre[h][0], pairs[2 * h]) for h in range(heads)]
    below = [dot_pairs(pairs[2 * h + 1], split2(inner[h])) for h in range(heads)]
    for h in range(heads):
        _, beta_row, grow_row, inv_row, tail, decay, c_row, g3 = pre[h]
        top = []
        bottom = []
        for which, data in ((0, keys[h]), (1, values[h])):
            scale = [beta_row[:, a * W : a * W + W] for a in range(2)]
            if which == 0:
                scale = [
                    scale[a] * grow_row[:, a * W : a * W + W] * inv_row[a] for a in range(2)
                ]
            t00 = split2(times_rows(inverse[2 * h], scale[0]))
            t10 = split2(times_rows(below[h], -scale[0]))
            t11 = split2(times_rows(inverse[2 * h + 1], scale[1]))
            d0, d1 = data[:W], data[W:]
            top.append(
                mm(jnp.concatenate(t00, axis=1), jnp.concatenate([d0, d0], axis=0))
            )
            bottom.append(
                mm(
                    jnp.concatenate([t10[0], t11[0], t10[1], t11[1]], axis=1),
                    jnp.concatenate([d0, d1, d0, d1], axis=0),
                )
            )
        write = jnp.concatenate(
            [jnp.concatenate(top, axis=1), jnp.concatenate(bottom, axis=1)], axis=0
        )
        turned = keys[h].astype(F32).T.astype(BF16)
        weighted = split2(jnp.concatenate([tail, tail], axis=1) * write)
        both = mm(jnp.concatenate([turned, turned], axis=1), jnp.concatenate(weighted, axis=0))
        move = jnp.where(row == col, decay, 0.0) - both[:, :W]
        out.append((move, both[:, W:], write, c_row, inv_row, g3))
    return out


def local_reads(query, key, made):
    _, _, write, c_row, inv_row, g3 = made
    row = iota((W, W), 0)
    col = iota((W, W), 1)
    upto = bits(col <= row)
    c_tok = mm_nt(jnp.concatenate([upto] * 3, axis=1), g3)
    seen = mm_nt(query, key)
    weights = []
    for a in range(2):
        cols = slice(a * W, a * W + W)
        diff = minus_rows(c_tok, c_row[:, cols])
        ratio = jnp.exp(jnp.where(col + a * W <= 2 * row + 1, diff, -1e30))
        weights.append(ratio * times_rows(seen[:, cols], inv_row[a]))
    both = x3(jnp.concatenate(weights, axis=1), write)
    return jnp.exp(c_tok) * query.astype(F32) - both[:, :W], both[:, W:]


def compose(later, earlier):
    move = dot_pairs(later[0], earlier[0])
    offset = dot_pairs(later[0], split2(earlier[1])) + later[1]
    return split2(move), offset


def kernel(
    n_y,
    n_tp,
    q_ref,
    k_ref,
    v_ref,
    beta_ref,
    gate_ref,
    gain_ref,
    w_ref,
    o_ref,
    k_buf,
    v_buf,
    w_buf,
    y_send,
    y_recv,
    l_send,
    l_recv,
    h_send,
    h_recv,
    pre_m,
    pre_n,
    state,
    r_send,
    r_recv,
    n_send,
    n_buf,
    w_ssem,
    w_rsem,
    w_lsem,
    y_ssem,
    y_rsem,
    l_ssem,
    l_rsem,
    h_ssem,
    h_rsem,
    r_ssem,
    r_rsem,
    n_ssem,
    n_rsem,
    f_ssem,
    i_sem,
    ready,
):
    ctx = lax.axis_index("ctx")
    tp = lax.axis_index("tp")
    y = lax.rem(ctx, n_y)
    z = ctx // n_y
    zl = lax.rem(z, 4)
    zg = z // 4
    core = lax.rem(tp, 2)
    wide = 512

    def at(zz, yy):
        return zz * n_y + yy

    loads = []
    for i, (ref, buf) in enumerate(((k_ref, k_buf), (v_ref, v_buf))):
        for h in range(2):
            copy = pltpu.make_async_copy(
                ref.reshape(2 * W, 2 * W).at[:, pl.ds(h * W, W)], buf.at[h], i_sem.at[2 * i + h]
            )
            copy.start()
            loads.append(copy)

    barrier = pltpu.get_barrier_semaphore()
    near = [(ctx, lax.rem(tp + d, n_tp)) for d in range(1, n_tp)]
    near += [
        (at(z, lax.rem(y + d, n_y)), lax.rem(tp + 2 * e, n_tp)) for d in range(1, n_y) for e in range(4)
    ]
    near += [(at(zg * 4 + lax.rem(zl + d, 4), y), tp) for d in range(1, 4)]
    for peer in near:
        pl.semaphore_signal(barrier, inc=1, device_id=peer, device_id_type=MESH)
    for d in range(1, 4):

        @pl.when(zg + d < 4)
        def _():
            pl.semaphore_signal(
                barrier, inc=1, device_id=(at(lax.rem(z + 4 * d, 16), y), tp), device_id_type=MESH
            )

    masks = make_masks()
    for copy in loads:
        copy.wait()
    keys = [k_buf[h] for h in range(2)]
    values = [v_buf[h] for h in range(2)]
    beta0 = [beta_ref[h : h + 1, :] for h in range(2)]
    beta1 = [beta_ref[2 + h : 3 + h, :] for h in range(2)]
    gates = [gate_ref[h : h + 1, :] for h in range(2)]

    pl.semaphore_wait(barrier, len(near) + zg)
    for d in range(1, 4):

        @pl.when(zg - d >= 0)
        def _():
            pl.semaphore_signal(
                ready, inc=1, device_id=(at(lax.rem(z + 16 - 4 * d, 16), y), tp),
                device_id_type=MESH,
            )

    def w_columns(owner):
        return w_ref.at[:, pl.ds(pl.multiple_of(owner * wide, wide), wide)]

    w_copies = []
    for d, flip in ((2, 0), (2, 1), (1, 0), (3, 0), (1, 1), (3, 1), (0, 1)):
        owner = lax.rem(tp // 2 + d, 4) * 2 + lax.rem(core + flip, 2)
        d = 2 * d + flip
        copy = pltpu.make_async_remote_copy(
            w_columns(owner), w_buf.at[tp], w_ssem.at[d], w_rsem.at[tp], (ctx, owner), MESH
        )
        copy.start()
        w_copies.append(copy)
    w_own = pltpu.make_async_copy(w_columns(tp), w_buf.at[tp], w_lsem)
    w_own.start()

    def y_copy(j):
        owner = 2 * core + j
        return pltpu.make_async_remote_copy(
            y_send.at[j], y_recv.at[y], y_ssem.at[j], y_rsem.at[y], (at(z, owner), tp), MESH
        )

    def r_copy(j):
        owner = 2 * core + j
        return pltpu.make_async_remote_copy(
            r_send.at[j], r_recv.at[y], r_ssem.at[j], r_rsem.at[y], (at(z, owner), tp), MESH
        )

    @pl.when(tp >= 0)
    def _():
        made = local_maps(masks, keys, values, beta0, beta1, gates)
        for j in range(2):
            move = split2(made[j][0])
            offset = made[j][1].astype(BF16)

            @pl.when(y == 2 * core + j)
            def _():
                y_recv[y, 0] = move[0]
                y_recv[y, 1] = move[1]
                y_recv[y, 2] = offset

            @pl.when(y != 2 * core + j)
            def _():
                y_send[j, 0] = move[0]
                y_send[j, 1] = move[1]
                y_send[j, 2] = offset
                y_copy(j).start()

        for j in range(2):
            eff, loc = local_reads(q_ref[:, j * W : j * W + W], keys[j], made[j])
            eff = eff.astype(BF16)
            loc = loc.astype(BF16)

            @pl.when(y == 2 * core + j)
            def _():
                r_recv[y, 0] = eff
                r_recv[y, 1] = loc

            @pl.when(y != 2 * core + j)
            def _():
                r_send[j, 0] = eff
                r_send[j, 1] = loc
                r_copy(j).start()

    def l_copy(d):
        other = lax.rem(zl + d, 4)
        return pltpu.make_async_remote_copy(
            l_send, l_recv.at[zl], l_ssem.at[d], l_rsem.at[zl], (at(zg * 4 + other, y), tp), MESH
        )

    def h_copy(d):
        return pltpu.make_async_remote_copy(
            h_send, h_recv.at[zg], h_ssem.at[d], h_rsem.at[zg],
            (at(lax.rem(z + 4 * d, 16), y), tp), MESH,
        )

    def h_copy_first(d):
        return pltpu.make_async_remote_copy(
            h_send.at[1], h_recv.at[0, 1], h_ssem.at[d], h_rsem.at[0],
            (at(lax.rem(z + 4 * d, 16), y), tp), MESH,
        )

    chip = tp // 2
    partner = chip * 2 + 1 - core

    def n_copy(dy, dx):
        s = lax.rem(y + dy, n_y)
        other = lax.rem(chip + dx, 4) * 2 + core
        return pltpu.make_async_remote_copy(
            n_send.at[s], n_buf.at[chip * 4 + y], n_ssem.at[dy * 4 + dx],
            n_rsem.at[chip * 4 + y], (at(z, s), other), MESH,
        )

    def ready_wait():
        @pl.when(zg < 3)
        def _():
            pl.semaphore_wait(ready, 3 - zg)

    @pl.when(y // 2 != core)
    def _():
        ready_wait()

    @pl.when(y // 2 == core)
    def _():
        for s in range(n_y):

            @pl.when(s != y)
            def _():
                pltpu.make_async_remote_copy(
                    y_recv.at[s], y_recv.at[s], y_ssem.at[0], y_rsem.at[s],
                    (at(z, s), tp), MESH,
                ).wait_recv()

        part = [
            ((y_recv[s, 0], y_recv[s, 1]), y_recv[s, 2].astype(F32)) for s in range(n_y)
        ]
        first_two = compose(part[1], part[0])
        last_two = compose(part[3], part[2])
        whole = compose(last_two, first_two)
        l_send[0] = whole[0][0]
        l_send[1] = whole[1].astype(BF16)
        for d in (3, 1, 2):
            l_copy(d).start()
        l_recv[zl, 0] = whole[0][0]
        l_recv[zl, 1] = whole[1].astype(BF16)
        for d in range(1, 4):
            src = lax.rem(zl + d, 4)
            pltpu.make_async_remote_copy(
                l_recv.at[src], l_recv.at[src], l_ssem.at[d], l_rsem.at[src],
                (at(zg * 4 + src, y), tp), MESH,
            ).wait_recv()
        none = jnp.zeros((W, W), BF16)
        grp = [((l_recv[s, 0], none), l_recv[s, 1].astype(F32)) for s in range(4)]
        low_two = compose(grp[1], grp[0])
        high_two = compose(grp[3], grp[2])
        total = compose(high_two, low_two)
        h_send[0] = total[0][0]
        h_send[1] = total[1].astype(BF16)
        ready_wait()
        @pl.when(zg == 0)
        def _():
            for d in (2, 3, 1):
                h_copy_first(d).start()

        for d in (2, 1):

            @pl.when((zg > 0) & (zg + d < 4))
            def _():
                h_copy(d).start()

        @pl.when(tp >= 0)
        def _():
            row = iota((W, W), 0)
            col = iota((W, W), 1)
            eye = (row == col).astype(F32)
            three = compose(part[2], first_two)
            low_three = compose(grp[2], low_two)

            def joined(pair):
                return pair[0].astype(F32) + pair[1].astype(F32)

            entry_m = jnp.where(
                zl == 0,
                eye,
                jnp.where(
                    zl == 1,
                    grp[0][0][0].astype(F32),
                    jnp.where(zl == 2, joined(low_two[0]), joined(low_three[0])),
                ),
            )
            entry_n = jnp.where(
                zl == 0,
                0.0,
                jnp.where(zl == 1, grp[0][1], jnp.where(zl == 2, low_two[1], low_three[1])),
            )
            entry = (split2(entry_m), entry_n)
            starts = [entry] + [compose(p, entry) for p in (part[0], first_two, three)]
            for s in range(n_y):

                @pl.when(s != y)
                def _():
                    pltpu.make_async_remote_copy(
                        r_recv.at[s], r_recv.at[s], r_ssem.at[0], r_rsem.at[s],
                        (at(z, s), tp), MESH,
                    ).wait_recv()

            for s in range(n_y):
                read = r_recv[s, 0]
                twice = jnp.concatenate([read, read], axis=1)
                move = split2(mm(twice, jnp.concatenate(starts[s][0], axis=0)))
                pre_m[s] = left3(move)
                pre_n[s] = mm(
                    twice, jnp.concatenate(split2(starts[s][1]), axis=0)
                ) + r_recv[s, 1].astype(F32)
            state[...] = jnp.zeros((W, W), F32)

        for s in range(3):

            @pl.when(s < zg)
            def _():
                if s == 0:
                    pltpu.make_async_remote_copy(
                        h_recv.at[0, 1], h_recv.at[0, 1], h_ssem.at[0], h_rsem.at[0],
                        (at(z, y), tp), MESH,
                    ).wait_recv()
                    state[...] = h_recv[0, 1].astype(F32)
                else:
                    pltpu.make_async_remote_copy(
                        h_recv.at[s], h_recv.at[s], h_ssem.at[0], h_rsem.at[s],
                        (at(z, y), tp), MESH,
                    ).wait_recv()
                    now = split2(state[...])
                    state[...] = mm(
                        jnp.concatenate([h_recv[s, 0], h_recv[s, 0]], axis=1),
                        jnp.concatenate([now[0], now[1]], axis=0),
                    ) + h_recv[s, 1].astype(F32)

        entering = right3(split2(state[...]))
        gain = jnp.where(
            lax.rem(y, 2) == 0, gain_ref[:, :W], gain_ref[:, W:]
        )
        for dy in (2, 1, 3, 0):
            s = lax.rem(y + dy, n_y)
            out = mm(pre_m[s], entering) + pre_n[s]
            scale = lax.rsqrt(jnp.mean(out * out, axis=1, keepdims=True) + 1e-06)
            done = (out * scale * gain).astype(BF16)
            n_send[s] = done
            if dy == 0:
                n_buf[chip * 4 + y] = done
            for dx in (2, 1, 3, 0):
                if dx or dy:
                    n_copy(dy, dx).start()

    def pass_on(j, dx):
        head = lax.rem(chip + dx, 4) * 4 + 2 * core + j
        return pltpu.make_async_remote_copy(
            n_buf.at[head], n_buf.at[head], f_ssem.at[j * 4 + dx], n_rsem.at[head],
            (ctx, partner), MESH,
        )

    def arrived(head):
        pltpu.make_async_remote_copy(
            n_buf.at[head], n_buf.at[head], f_ssem.at[0], n_rsem.at[head], (ctx, partner), MESH
        ).wait_recv()

    def w_arrived(src):
        pltpu.make_async_remote_copy(
            w_buf.at[src], w_buf.at[src], w_ssem.at[0], w_rsem.at[src], (ctx, partner), MESH
        ).wait_recv()

    def term(first, src):
        both = jnp.concatenate([n_buf[first], n_buf[first + 1]], axis=1)
        return mm(both, w_buf[src])

    total = None
    for dx in (0, 1, 3, 2):
        src = lax.rem(chip + dx, 4) * 2 + core
        first = lax.rem(chip + dx, 4) * 4 + 2 * core
        for j in range(2):
            if dx == 0:

                @pl.when(y != 2 * core + j)
                def _():
                    arrived(first + j)

            else:
                arrived(first + j)
            pass_on(j, dx).start()
        if dx == 0:
            w_own.wait()
        else:
            w_arrived(src)
        part = term(first, src)
        total = part if total is None else total + part
    for dx in (0, 1, 3, 2):
        src = lax.rem(chip + dx, 4) * 2 + 1 - core
        first = lax.rem(chip + dx, 4) * 4 + 2 * (1 - core)
        w_arrived(src)
        arrived(first)
        arrived(first + 1)
        total = total + term(first, src)
    o_ref[...] = total.astype(BF16)

    for copy in w_copies:
        copy.wait_send()
    for j in range(2):
        for dx in range(4):
            pass_on(j, dx).wait_send()

        @pl.when(y != 2 * core + j)
        def _():
            y_copy(j).wait_send()
            r_copy(j).wait_send()

    @pl.when(y // 2 == core)
    def _():
        for d in range(1, 4):
            l_copy(d).wait_send()

            @pl.when(zg == 0)
            def _():
                h_copy_first(d).wait_send()

            @pl.when((zg > 0) & (zg + d < 4))
            def _():
                h_copy(d).wait_send()

        for dy in range(n_y):
            for dx in range(4):
                if dx or dy:
                    n_copy(dy, dx).wait_send()


def local(queries, key_vectors, value_vectors, strengths, log_gate, out_gain, out_weight):
    tokens = queries.shape[0]
    n_tp = 8
    n_y = 4
    width = out_weight.shape[1] // n_tp
    vmem = pl.BlockSpec(memory_space=pltpu.VMEM)
    hbm = pl.BlockSpec(memory_space=pl.ANY)
    dma = pltpu.SemaphoreType.DMA
    return pl.pallas_call(
        functools.partial(kernel, n_y, n_tp),
        out_shape=jax.ShapeDtypeStruct((tokens, width), BF16),
        in_specs=[vmem, hbm, hbm, vmem, vmem, vmem, hbm],
        out_specs=vmem,
        scratch_shapes=[
            pltpu.VMEM((2, 2 * W, W), BF16),
            pltpu.VMEM((2, 2 * W, W), BF16),
            pltpu.VMEM((n_tp, 2 * W, width), BF16),
            pltpu.VMEM((2, 3, W, W), BF16),
            pltpu.VMEM((n_y, 3, W, W), BF16),
            pltpu.VMEM((2, W, W), BF16),
            pltpu.VMEM((4, 2, W, W), BF16),
            pltpu.VMEM((2, W, W), BF16),
            pltpu.VMEM((4, 2, W, W), BF16),
            pltpu.VMEM((n_y, W, 3 * W), BF16),
            pltpu.VMEM((n_y, W, W), F32),
            pltpu.VMEM((W, W), F32),
            pltpu.VMEM((2, 2, W, W), BF16),
            pltpu.VMEM((n_y, 2, W, W), BF16),
            pltpu.VMEM((n_y, W, W), BF16),
            pltpu.VMEM((2 * n_tp, W, W), BF16),
            dma((n_tp,)),
            dma((n_tp,)),
            dma,
            dma((2,)),
            dma((n_y,)),
            dma((4,)),
            dma((4,)),
            dma((4,)),
            dma((4,)),
            dma((2,)),
            dma((n_y,)),
            dma((16,)),
            dma((16,)),
            dma((8,)),
            dma((4,)),
            pltpu.SemaphoreType.REGULAR,
        ],
        compiler_params=pltpu.CompilerParams(collective_id=0, has_side_effects=True),
    )(
        queries,
        key_vectors,
        value_vectors,
        strengths.reshape(4, tokens),
        log_gate,
        out_gain.reshape(1, -1),
        out_weight,
    )


def solution(mesh):
    placed = (
        P("ctx", "tp"),
        P("ctx", None, "tp"),
        P("ctx", None, "tp"),
        P(None, "tp", "ctx"),
        P("tp", "ctx"),
        P("tp"),
        P("tp", None),
    )
    return jax.shard_map(
        local, mesh=mesh, in_specs=placed, out_specs=P("ctx", "tp"), check_vma=False
    )
```

```python
import functools

import jax
import jax.numpy as jnp
from jax import lax
from jax.experimental import pallas as pl
from jax.experimental.pallas import tpu as pltpu
from jax.sharding import PartitionSpec as P

MESH = pl.DeviceIdType.MESH
F32 = jnp.float32
BF16 = jnp.bfloat16
W = 128


def mm(a, b):
    return jnp.dot(a, b, preferred_element_type=F32)


def mm_nt(a, b):
    return lax.dot_general(a, b, (((1,), (1,)), ((), ())), preferred_element_type=F32)


def split2(a):
    hi = a.astype(BF16)
    return hi, (a - hi.astype(F32)).astype(BF16)


def split3(a):
    hi = a.astype(BF16)
    rest = a - hi.astype(F32)
    mid = rest.astype(BF16)
    return hi, mid, (rest - mid.astype(F32)).astype(BF16)


def left3(pair):
    return jnp.concatenate([pair[0], pair[1], pair[0]], axis=1)


def right3(pair):
    return jnp.concatenate([pair[0], pair[0], pair[1]], axis=0)


def dot_pairs(a, b):
    return mm(left3(a), right3(b))


def dot_pair_one(a, b):
    return mm(jnp.concatenate([a[0], a[1]], axis=1), jnp.concatenate([b, b], axis=0))


def x3(a, b):
    return dot_pairs(split2(a), split2(b))


def iota(shape, dim):
    return lax.broadcasted_iota(jnp.int32, shape, dim)


def bits(mask):
    return mask.astype(F32).astype(BF16)


def by_rows(block, rows):
    n = block.shape[0]
    return block.reshape(n // 8, 8, W), jnp.broadcast_to(rows[None], (n // 8, 8, W))


def times_rows(block, rows):
    a, b = by_rows(block, rows)
    return (a * b).reshape(block.shape)


def minus_rows(block, rows):
    a, b = by_rows(block, rows)
    return (a - b).reshape(block.shape)


def make_masks():
    step = iota((2 * W, W), 0)
    token = iota((2 * W, W), 1)
    row = iota((W, W), 0)
    col = iota((W, W), 1)
    upto = bits(2 * token <= step)
    first = bits(2 * token == step)
    second = bits(2 * token + 1 == step)
    levels = []
    size = 1
    while size < W:
        levels.append(bits((row // size == col // size + 1) & ((row // size) % 2 == 1)))
        size *= 2
    return (
        jnp.concatenate([upto] * 3, axis=1),
        jnp.concatenate([first] * 3 + [second] * 3, axis=1),
        levels,
    )


def local_maps(masks, keys, values, beta0, beta1, gate):
    heads = len(keys)
    upto3, pick, levels = masks
    row = iota((W, W), 0)
    col = iota((W, W), 1)
    eye = (row == col).astype(F32)
    pre = []
    low = []
    for h in range(heads):
        k = keys[h]
        k32 = k.astype(F32)
        gram = mm_nt(k, k)
        inv_col = lax.rsqrt(jnp.sum(k32 * k32, axis=1, keepdims=True) + 1e-06)
        inv_row = []
        for a in range(2):
            part = jnp.where(row == col, gram[a * W : a * W + W, a * W : a * W + W], 0.0)
            total = jnp.sum(part.reshape(W // 8, 8, W), axis=0)
            total = jnp.broadcast_to(jnp.sum(total, axis=0, keepdims=True), (8, W))
            inv_row.append(lax.rsqrt(total + 1e-06))
        g3 = jnp.concatenate(split3(jnp.broadcast_to(gate[h], (W, W))), axis=1)
        b3 = jnp.concatenate(
            split3(jnp.broadcast_to(beta0[h], (W, W))) + split3(jnp.broadcast_to(beta1[h], (W, W))),
            axis=1,
        )
        c_col = mm_nt(upto3, g3)
        c_row = mm_nt(g3[:8], upto3)
        beta = mm_nt(pick, b3)
        beta_row = mm_nt(b3[:8], pick)
        grow_row = jnp.exp(c_row)
        scaled = beta * inv_col
        blocks = {}
        for a, b in ((0, 0), (1, 1), (1, 0)):
            ra, cb = slice(a * W, a * W + W), slice(b * W, b * W + W)
            diff = minus_rows(c_col[ra], c_row[:, cb])
            if a == b:
                diff = jnp.where(row > col, diff, -1e30)
            block = scaled[ra] * jnp.exp(diff) * times_rows(gram[ra, cb], inv_row[b])
            blocks[a, b] = split2(block)
        last = c_col[2 * W - 1 : 2 * W]
        tail = inv_col * jnp.exp(last - c_col)
        pre.append((blocks[1, 0], beta_row, grow_row, inv_row, tail, jnp.exp(last), c_row, g3))
        low += [blocks[0, 0], blocks[1, 1]]
    inverse = [
        eye - (part[0] * levels[0]).astype(F32) - (part[1] * levels[0]).astype(F32) for part in low
    ]
    for mask in levels[1:]:
        pairs = [split2(t) for t in inverse]
        inner = [
            dot_pairs((part[0] * mask, part[1] * mask), pair) for part, pair in zip(low, pairs)
        ]
        inverse = [t - dot_pairs(pair, split2(c)) for t, pair, c in zip(inverse, pairs, inner)]
    out = []
    pairs = [split2(t) for t in inverse]
    inner = [dot_pairs(pre[h][0], pairs[2 * h]) for h in range(heads)]
    below = [dot_pairs(pairs[2 * h + 1], split2(inner[h])) for h in range(heads)]
    for h in range(heads):
        _, beta_row, grow_row, inv_row, tail, decay, c_row, g3 = pre[h]
        top = []
        bottom = []
        for which, data in ((0, keys[h]), (1, values[h])):
            scale = [beta_row[:, a * W : a * W + W] for a in range(2)]
            if which == 0:
                scale = [
                    scale[a] * grow_row[:, a * W : a * W + W] * inv_row[a] for a in range(2)
                ]
            t00 = split2(times_rows(inverse[2 * h], scale[0]))
            t10 = split2(times_rows(below[h], -scale[0]))
            t11 = split2(times_rows(inverse[2 * h + 1], scale[1]))
            d0, d1 = data[:W], data[W:]
            top.append(
                mm(jnp.concatenate(t00, axis=1), jnp.concatenate([d0, d0], axis=0))
            )
            bottom.append(
                mm(
                    jnp.concatenate([t10[0], t11[0], t10[1], t11[1]], axis=1),
                    jnp.concatenate([d0, d1, d0, d1], axis=0),
                )
            )
        write = jnp.concatenate(
            [jnp.concatenate(top, axis=1), jnp.concatenate(bottom, axis=1)], axis=0
        )
        turned = keys[h].astype(F32).T.astype(BF16)
        weighted = split2(jnp.concatenate([tail, tail], axis=1) * write)
        both = mm(jnp.concatenate([turned, turned], axis=1), jnp.concatenate(weighted, axis=0))
        move = jnp.where(row == col, decay, 0.0) - both[:, :W]
        out.append((move, both[:, W:], write, c_row, inv_row, g3))
    return out


def local_reads(query, key, gate, write, c_row, inv_rows):
    g3 = jnp.concatenate(split3(jnp.broadcast_to(gate, (W, W))), axis=1)
    row = iota((W, W), 0)
    col = iota((W, W), 1)
    upto = bits(col <= row)
    c_tok = mm_nt(jnp.concatenate([upto] * 3, axis=1), g3)
    seen = mm_nt(query, key)
    weights = []
    for a in range(2):
        cols = slice(a * W, a * W + W)
        diff = minus_rows(c_tok, c_row[:, cols])
        ratio = jnp.exp(jnp.where(col + a * W <= 2 * row + 1, diff, -1e30))
        weights.append(ratio * times_rows(seen[:, cols], inv_rows[:, cols]))
    both = dot_pairs(split2(jnp.concatenate(weights, axis=1)), write)
    return jnp.exp(c_tok) * query.astype(F32) - both[:, :W], both[:, W:]


def apply(left, right):
    if left[1] is None and right[1] is None:
        return mm(left[0], right[0])
    if left[1] is None:
        return mm(
            jnp.concatenate([left[0], left[0]], axis=1), jnp.concatenate(right, axis=0)
        )
    if right[1] is None:
        return dot_pair_one(left, right[0])
    return dot_pairs(left, right)


def compose(later, earlier):
    move = apply(later[0], earlier[0])
    offset = apply(later[0], split2(earlier[1])) + later[1]
    return split2(move), offset


def kernel(
    n_y,
    n_tp,
    q_hbm,
    k_hbm,
    v_hbm,
    beta_hbm,
    gate_hbm,
    gain_hbm,
    w_ref,
    o_ref,
    k_buf,
    v_buf,
    q_ref,
    beta_ref,
    gate_ref,
    gain_ref,
    written,
    rows_buf,
    w_buf,
    y_send,
    y_recv,
    l_send,
    l_recv,
    h_send,
    h_recv,
    pre_m,
    pre_n,
    state,
    r_send,
    r_recv,
    n_send,
    n_buf,
    w_ssem,
    w_rsem,
    w_lsem,
    y_ssem,
    y_rsem,
    l_ssem,
    l_rsem,
    h_ssem,
    h_rsem,
    r_ssem,
    r_rsem,
    n_ssem,
    n_rsem,
    f_ssem,
    i_sem,
    ready,
):
    ctx = lax.axis_index("ctx")
    tp = lax.axis_index("tp")
    y = lax.rem(ctx, n_y)
    z = ctx // n_y
    zl = lax.rem(z, 4)
    zg = z // 4
    core = lax.rem(tp, 2)
    wide = 512

    def at(zz, yy):
        return zz * n_y + yy

    loads = []
    for i, (ref, buf) in enumerate(((k_hbm, k_buf), (v_hbm, v_buf))):
        for h in range(2):
            copy = pltpu.make_async_copy(
                ref.reshape(2 * W, 2 * W).at[:, pl.ds(h * W, W)], buf.at[h], i_sem.at[2 * i + h]
            )
            copy.start()
            loads.append(copy)

    for i, (ref, buf) in enumerate(
        ((beta_hbm, beta_ref), (gate_hbm, gate_ref), (q_hbm, q_ref), (gain_hbm, gain_ref))
    ):
        copy = pltpu.make_async_copy(ref, buf, i_sem.at[4 + i])
        copy.start()
        loads.append(copy)

    barrier = pltpu.get_barrier_semaphore()
    near = [(ctx, lax.rem(tp + d, n_tp)) for d in range(1, n_tp)]
    near += [
        (at(z, lax.rem(y + d, n_y)), lax.rem(tp + 2 * e, n_tp)) for d in range(1, n_y) for e in range(4)
    ]
    near += [(at(zg * 4 + lax.rem(zl + d, 4), y), tp) for d in range(1, 4)]
    for peer in near:
        pl.semaphore_signal(barrier, inc=1, device_id=peer, device_id_type=MESH)
    for d in range(1, 4):

        @pl.when(zg + d < 4)
        def _():
            pl.semaphore_signal(
                barrier, inc=1, device_id=(at(lax.rem(z + 4 * d, 16), y), tp), device_id_type=MESH
            )

    masks = make_masks()
    for copy in loads:
        copy.wait()
    keys = [k_buf[h] for h in range(2)]
    values = [v_buf[h] for h in range(2)]
    beta0 = [beta_ref[h : h + 1, :] for h in range(2)]
    beta1 = [beta_ref[2 + h : 3 + h, :] for h in range(2)]
    gates = [gate_ref[h : h + 1, :] for h in range(2)]

    def y_copy(j):
        owner = 2 * core + j
        return pltpu.make_async_remote_copy(
            y_send.at[j], y_recv.at[y], y_ssem.at[j], y_rsem.at[y], (at(z, owner), tp), MESH
        )

    def r_copy(j):
        owner = 2 * core + j
        return pltpu.make_async_remote_copy(
            r_send.at[j], r_recv.at[y], r_ssem.at[j], r_rsem.at[y], (at(z, owner), tp), MESH
        )

    @pl.when(tp >= 0)
    def _():
        made = local_maps(masks, keys, values, beta0, beta1, gates)
        for j in range(2):
            move = made[j][0].astype(BF16)
            offset = made[j][1].astype(BF16)
            hi, lo = split2(made[j][2])
            written[j, 0] = hi
            written[j, 1] = lo
            rows_buf[j, 0] = made[j][3]
            rows_buf[j, 1] = jnp.concatenate(made[j][4], axis=1)

            @pl.when(y == 2 * core + j)
            def _():
                y_recv[y, 0] = move
                y_recv[y, 1] = offset

            @pl.when(y != 2 * core + j)
            def _():
                y_send[j, 0] = move
                y_send[j, 1] = offset

    pl.semaphore_wait(barrier, len(near) + zg)
    for d in range(1, 4):

        @pl.when(zg - d >= 0)
        def _():
            pl.semaphore_signal(
                ready, inc=1, device_id=(at(lax.rem(z + 16 - 4 * d, 16), y), tp),
                device_id_type=MESH,
            )

    for j in range(2):

        @pl.when(y != 2 * core + j)
        def _():
            y_copy(j).start()

    def w_columns(owner):
        return w_ref.at[:, pl.ds(pl.multiple_of(owner * wide, wide), wide)]

    w_copies = []
    for d, flip in ((2, 0), (2, 1), (1, 0), (3, 0), (1, 1), (3, 1), (0, 1)):
        owner = lax.rem(tp // 2 + d, 4) * 2 + lax.rem(core + flip, 2)
        d = 2 * d + flip
        copy = pltpu.make_async_remote_copy(
            w_columns(owner), w_buf.at[tp], w_ssem.at[d], w_rsem.at[tp], (ctx, owner), MESH
        )
        copy.start()
        w_copies.append(copy)
    w_own = pltpu.make_async_copy(w_columns(tp), w_buf.at[tp], w_lsem)
    w_own.start()

    @pl.when(tp >= 0)
    def _():
        for j in range(2):
            eff, loc = local_reads(
                q_ref[:, j * W : j * W + W], k_buf[j], gate_ref[j : j + 1, :],
                (written[j, 0], written[j, 1]), rows_buf[j, 0], rows_buf[j, 1],
            )
            eff = eff.astype(BF16)
            loc = loc.astype(BF16)

            @pl.when(y == 2 * core + j)
            def _():
                r_recv[y, 0] = eff
                r_recv[y, 1] = loc

            @pl.when(y != 2 * core + j)
            def _():
                r_send[j, 0] = eff
                r_send[j, 1] = loc
                r_copy(j).start()

    def l_copy(d):
        other = lax.rem(zl + d, 4)
        return pltpu.make_async_remote_copy(
            l_send, l_recv.at[zl], l_ssem.at[d], l_rsem.at[zl], (at(zg * 4 + other, y), tp), MESH
        )

    def h_copy(d):
        return pltpu.make_async_remote_copy(
            h_send, h_recv.at[zg], h_ssem.at[d], h_rsem.at[zg],
            (at(lax.rem(z + 4 * d, 16), y), tp), MESH,
        )

    def h_copy_first(d):
        return pltpu.make_async_remote_copy(
            h_send.at[1], h_recv.at[0, 1], h_ssem.at[d], h_rsem.at[0],
            (at(lax.rem(z + 4 * d, 16), y), tp), MESH,
        )

    chip = tp // 2
    partner = chip * 2 + 1 - core

    def n_copy(dy, dx):
        s = lax.rem(y + dy, n_y)
        other = lax.rem(chip + dx, 4) * 2 + core
        return pltpu.make_async_remote_copy(
            n_send.at[s], n_buf.at[chip * 4 + y], n_ssem.at[dy * 4 + dx],
            n_rsem.at[chip * 4 + y], (at(z, s), other), MESH,
        )

    def ready_wait():
        @pl.when(zg < 3)
        def _():
            pl.semaphore_wait(ready, 3 - zg)

    @pl.when(y // 2 != core)
    def _():
        ready_wait()

    @pl.when(y // 2 == core)
    def _():
        for s in range(n_y):

            @pl.when(s != y)
            def _():
                pltpu.make_async_remote_copy(
                    y_recv.at[s], y_recv.at[s], y_ssem.at[0], y_rsem.at[s],
                    (at(z, s), tp), MESH,
                ).wait_recv()

        part = [
            ((y_recv[s, 0], None), y_recv[s, 1].astype(F32)) for s in range(n_y)
        ]
        first_two = compose(part[1], part[0])
        last_two = compose(part[3], part[2])
        whole = compose(last_two, first_two)
        l_send[0] = whole[0][0]
        l_send[1] = whole[1].astype(BF16)
        for d in (3, 1, 2):
            l_copy(d).start()
        l_recv[zl, 0] = whole[0][0]
        l_recv[zl, 1] = whole[1].astype(BF16)
        for d in range(1, 4):
            src = lax.rem(zl + d, 4)
            pltpu.make_async_remote_copy(
                l_recv.at[src], l_recv.at[src], l_ssem.at[d], l_rsem.at[src],
                (at(zg * 4 + src, y), tp), MESH,
            ).wait_recv()
        grp = [((l_recv[s, 0], None), l_recv[s, 1].astype(F32)) for s in range(4)]
        low_two = compose(grp[1], grp[0])
        high_two = compose(grp[3], grp[2])
        total = compose(high_two, low_two)
        h_send[0] = total[0][0]
        h_send[1] = total[1].astype(BF16)
        ready_wait()
        @pl.when(zg == 0)
        def _():
            for d in (2, 3, 1):
                h_copy_first(d).start()

        for d in (2, 1):

            @pl.when((zg > 0) & (zg + d < 4))
            def _():
                h_copy(d).start()

        @pl.when(tp >= 0)
        def _():
            row = iota((W, W), 0)
            col = iota((W, W), 1)
            eye = (row == col).astype(F32)
            three = compose(part[2], first_two)
            low_three = compose(grp[2], low_two)

            def joined(pair):
                return pair[0].astype(F32) + pair[1].astype(F32)

            entry_m = jnp.where(
                zl == 0,
                eye,
                jnp.where(
                    zl == 1,
                    grp[0][0][0].astype(F32),
                    jnp.where(zl == 2, joined(low_two[0]), joined(low_three[0])),
                ),
            )
            entry_n = jnp.where(
                zl == 0,
                0.0,
                jnp.where(zl == 1, grp[0][1], jnp.where(zl == 2, low_two[1], low_three[1])),
            )
            entry = (split2(entry_m), entry_n)
            starts = [entry] + [compose(p, entry) for p in (part[0], first_two, three)]
            for s in range(n_y):

                @pl.when(s != y)
                def _():
                    pltpu.make_async_remote_copy(
                        r_recv.at[s], r_recv.at[s], r_ssem.at[0], r_rsem.at[s],
                        (at(z, s), tp), MESH,
                    ).wait_recv()

            for s in range(n_y):
                read = r_recv[s, 0]
                twice = jnp.concatenate([read, read], axis=1)
                move = split2(mm(twice, jnp.concatenate(starts[s][0], axis=0)))
                pre_m[s] = left3(move)
                pre_n[s] = mm(
                    twice, jnp.concatenate(split2(starts[s][1]), axis=0)
                ) + r_recv[s, 1].astype(F32)
            state[...] = jnp.zeros((W, W), F32)

        for s in range(3):

            @pl.when(s < zg)
            def _():
                if s == 0:
                    pltpu.make_async_remote_copy(
                        h_recv.at[0, 1], h_recv.at[0, 1], h_ssem.at[0], h_rsem.at[0],
                        (at(z, y), tp), MESH,
                    ).wait_recv()
                    state[...] = h_recv[0, 1].astype(F32)
                else:
                    pltpu.make_async_remote_copy(
                        h_recv.at[s], h_recv.at[s], h_ssem.at[0], h_rsem.at[s],
                        (at(z, y), tp), MESH,
                    ).wait_recv()
                    now = split2(state[...])
                    state[...] = mm(
                        jnp.concatenate([h_recv[s, 0], h_recv[s, 0]], axis=1),
                        jnp.concatenate([now[0], now[1]], axis=0),
                    ) + h_recv[s, 1].astype(F32)

        entering = right3(split2(state[...]))
        gain = jnp.where(
            lax.rem(y, 2) == 0, gain_ref[:, :W], gain_ref[:, W:]
        )
        for dy in (2, 1, 3, 0):
            s = lax.rem(y + dy, n_y)
            out = mm(pre_m[s], entering) + pre_n[s]
            scale = lax.rsqrt(jnp.mean(out * out, axis=1, keepdims=True) + 1e-06)
            done = (out * scale * gain).astype(BF16)
            n_send[s] = done
            if dy == 0:
                n_buf[chip * 4 + y] = done
            for dx in (2, 1, 3, 0):
                if dx or dy:
                    n_copy(dy, dx).start()

    def pass_on(j, dx):
        head = lax.rem(chip + dx, 4) * 4 + 2 * core + j
        return pltpu.make_async_remote_copy(
            n_buf.at[head], n_buf.at[head], f_ssem.at[j * 4 + dx], n_rsem.at[head],
            (ctx, partner), MESH,
        )

    def arrived(head):
        pltpu.make_async_remote_copy(
            n_buf.at[head], n_buf.at[head], f_ssem.at[0], n_rsem.at[head], (ctx, partner), MESH
        ).wait_recv()

    def w_arrived(src):
        pltpu.make_async_remote_copy(
            w_buf.at[src], w_buf.at[src], w_ssem.at[0], w_rsem.at[src], (ctx, partner), MESH
        ).wait_recv()

    def term(first, src):
        both = jnp.concatenate([n_buf[first], n_buf[first + 1]], axis=1)
        return mm(both, w_buf[src])

    total = None
    for dx in (0, 1, 3, 2):
        src = lax.rem(chip + dx, 4) * 2 + core
        first = lax.rem(chip + dx, 4) * 4 + 2 * core
        for j in range(2):
            if dx == 0:

                @pl.when(y != 2 * core + j)
                def _():
                    arrived(first + j)

            else:
                arrived(first + j)
            pass_on(j, dx).start()
        if dx == 0:
            w_own.wait()
        else:
            w_arrived(src)
        part = term(first, src)
        total = part if total is None else total + part
    for dx in (0, 1, 3, 2):
        src = lax.rem(chip + dx, 4) * 2 + 1 - core
        first = lax.rem(chip + dx, 4) * 4 + 2 * (1 - core)
        w_arrived(src)
        arrived(first)
        arrived(first + 1)
        total = total + term(first, src)
    o_ref[...] = total.astype(BF16)

    for copy in w_copies:
        copy.wait_send()
    for j in range(2):
        for dx in range(4):
            pass_on(j, dx).wait_send()

        @pl.when(y != 2 * core + j)
        def _():
            y_copy(j).wait_send()
            r_copy(j).wait_send()

    @pl.when(y // 2 == core)
    def _():
        for d in range(1, 4):
            l_copy(d).wait_send()

            @pl.when(zg == 0)
            def _():
                h_copy_first(d).wait_send()

            @pl.when((zg > 0) & (zg + d < 4))
            def _():
                h_copy(d).wait_send()

        for dy in range(n_y):
            for dx in range(4):
                if dx or dy:
                    n_copy(dy, dx).wait_send()


def local(queries, key_vectors, value_vectors, strengths, log_gate, out_gain, out_weight):
    tokens = queries.shape[0]
    n_tp = 8
    n_y = 4
    width = out_weight.shape[1] // n_tp
    vmem = pl.BlockSpec(memory_space=pltpu.VMEM)
    hbm = pl.BlockSpec(memory_space=pl.ANY)
    dma = pltpu.SemaphoreType.DMA
    return pl.pallas_call(
        functools.partial(kernel, n_y, n_tp),
        out_shape=jax.ShapeDtypeStruct((tokens, width), BF16),
        in_specs=[hbm] * 7,
        out_specs=vmem,
        scratch_shapes=[
            pltpu.VMEM((2, 2 * W, W), BF16),
            pltpu.VMEM((2, 2 * W, W), BF16),
            pltpu.VMEM((W, 2 * W), BF16),
            pltpu.VMEM((4, W), F32),
            pltpu.VMEM((2, W), F32),
            pltpu.VMEM((1, 2 * W), F32),
            pltpu.VMEM((2, 2, 2 * W, 2 * W), BF16),
            pltpu.VMEM((2, 2, 8, 2 * W), F32),
            pltpu.VMEM((n_tp, 2 * W, width), BF16),
            pltpu.VMEM((2, 2, W, W), BF16),
            pltpu.VMEM((n_y, 2, W, W), BF16),
            pltpu.VMEM((2, W, W), BF16),
            pltpu.VMEM((4, 2, W, W), BF16),
            pltpu.VMEM((2, W, W), BF16),
            pltpu.VMEM((4, 2, W, W), BF16),
            pltpu.VMEM((n_y, W, 3 * W), BF16),
            pltpu.VMEM((n_y, W, W), F32),
            pltpu.VMEM((W, W), F32),
            pltpu.VMEM((2, 2, W, W), BF16),
            pltpu.VMEM((n_y, 2, W, W), BF16),
            pltpu.VMEM((n_y, W, W), BF16),
            pltpu.VMEM((2 * n_tp, W, W), BF16),
            dma((n_tp,)),
            dma((n_tp,)),
            dma,
            dma((2,)),
            dma((n_y,)),
            dma((4,)),
            dma((4,)),
            dma((4,)),
            dma((4,)),
            dma((2,)),
            dma((n_y,)),
            dma((16,)),
            dma((16,)),
            dma((8,)),
            dma((8,)),
            pltpu.SemaphoreType.REGULAR,
        ],
        compiler_params=pltpu.CompilerParams(collective_id=0, has_side_effects=True),
    )(
        queries,
        key_vectors,
        value_vectors,
        strengths.reshape(4, tokens),
        log_gate,
        out_gain.reshape(1, -1),
        out_weight,
    )


def solution(mesh):
    placed = (
        P("ctx", "tp"),
        P("ctx", None, "tp"),
        P("ctx", None, "tp"),
        P(None, "tp", "ctx"),
        P("tp", "ctx"),
        P("tp"),
        P("tp", None),
    )
    return jax.shard_map(
        local, mesh=mesh, in_specs=placed, out_specs=P("ctx", "tp"), check_vma=False
    )
```

```python
import functools

import jax
import jax.numpy as jnp
from jax import lax
from jax.experimental import pallas as pl
from jax.experimental.pallas import tpu as pltpu
from jax.sharding import PartitionSpec as P

MESH = pl.DeviceIdType.MESH
F32 = jnp.float32
BF16 = jnp.bfloat16
W = 128


def mm(a, b):
    return jnp.dot(a, b, preferred_element_type=F32)


def mm_nt(a, b):
    return lax.dot_general(a, b, (((1,), (1,)), ((), ())), preferred_element_type=F32)


def split2(a):
    hi = a.astype(BF16)
    return hi, (a - hi.astype(F32)).astype(BF16)


def split3(a):
    hi = a.astype(BF16)
    rest = a - hi.astype(F32)
    mid = rest.astype(BF16)
    return hi, mid, (rest - mid.astype(F32)).astype(BF16)


def left3(pair):
    return jnp.concatenate([pair[0], pair[1], pair[0]], axis=1)


def right3(pair):
    return jnp.concatenate([pair[0], pair[0], pair[1]], axis=0)


def dot_pairs(a, b):
    return mm(left3(a), right3(b))


def dot_pair_one(a, b):
    return mm(jnp.concatenate([a[0], a[1]], axis=1), jnp.concatenate([b, b], axis=0))


def x3(a, b):
    return dot_pairs(split2(a), split2(b))


def iota(shape, dim):
    return lax.broadcasted_iota(jnp.int32, shape, dim)


def bits(mask):
    return mask.astype(F32).astype(BF16)


def by_rows(block, rows):
    n = block.shape[0]
    return block.reshape(n // 8, 8, W), jnp.broadcast_to(rows[None], (n // 8, 8, W))


def times_rows(block, rows):
    a, b = by_rows(block, rows)
    return (a * b).reshape(block.shape)


def minus_rows(block, rows):
    a, b = by_rows(block, rows)
    return (a - b).reshape(block.shape)


def make_masks():
    step = iota((2 * W, W), 0)
    token = iota((2 * W, W), 1)
    row = iota((W, W), 0)
    col = iota((W, W), 1)
    upto = bits(2 * token <= step)
    first = bits(2 * token == step)
    second = bits(2 * token + 1 == step)
    levels = []
    size = 1
    while size < W:
        levels.append(bits((row // size == col // size + 1) & ((row // size) % 2 == 1)))
        size *= 2
    return (
        jnp.concatenate([upto] * 3, axis=1),
        jnp.concatenate([first] * 3 + [second] * 3, axis=1),
        levels,
    )


def local_maps(masks, keys, values, beta0, beta1, gate):
    heads = len(keys)
    upto3, pick, levels = masks
    row = iota((W, W), 0)
    col = iota((W, W), 1)
    eye = (row == col).astype(F32)
    pre = []
    low = []
    for h in range(heads):
        k = keys[h]
        k32 = k.astype(F32)
        gram = mm_nt(k, k)
        inv_col = lax.rsqrt(jnp.sum(k32 * k32, axis=1, keepdims=True) + 1e-06)
        inv_row = []
        for a in range(2):
            part = jnp.where(row == col, gram[a * W : a * W + W, a * W : a * W + W], 0.0)
            total = jnp.sum(part.reshape(W // 8, 8, W), axis=0)
            total = jnp.broadcast_to(jnp.sum(total, axis=0, keepdims=True), (8, W))
            inv_row.append(lax.rsqrt(total + 1e-06))
        g3 = jnp.concatenate(split3(jnp.broadcast_to(gate[h], (W, W))), axis=1)
        b3 = jnp.concatenate(
            split3(jnp.broadcast_to(beta0[h], (W, W))) + split3(jnp.broadcast_to(beta1[h], (W, W))),
            axis=1,
        )
        c_col = mm_nt(upto3, g3)
        c_row = mm_nt(g3[:8], upto3)
        beta = mm_nt(pick, b3)
        beta_row = mm_nt(b3[:8], pick)
        grow_row = jnp.exp(c_row)
        scaled = beta * inv_col
        blocks = {}
        for a, b in ((0, 0), (1, 1), (1, 0)):
            ra, cb = slice(a * W, a * W + W), slice(b * W, b * W + W)
            diff = minus_rows(c_col[ra], c_row[:, cb])
            if a == b:
                diff = jnp.where(row > col, diff, -1e30)
            block = scaled[ra] * jnp.exp(diff) * times_rows(gram[ra, cb], inv_row[b])
            blocks[a, b] = split2(block)
        last = c_col[2 * W - 1 : 2 * W]
        tail = inv_col * jnp.exp(last - c_col)
        pre.append((blocks[1, 0], beta_row, grow_row, inv_row, tail, jnp.exp(last), c_row, g3))
        low += [blocks[0, 0], blocks[1, 1]]
    inverse = [
        eye - (part[0] * levels[0]).astype(F32) - (part[1] * levels[0]).astype(F32) for part in low
    ]
    for mask in levels[1:]:
        pairs = [split2(t) for t in inverse]
        inner = [
            dot_pairs((part[0] * mask, part[1] * mask), pair) for part, pair in zip(low, pairs)
        ]
        inverse = [t - dot_pairs(pair, split2(c)) for t, pair, c in zip(inverse, pairs, inner)]
    out = []
    pairs = [split2(t) for t in inverse]
    inner = [dot_pairs(pre[h][0], pairs[2 * h]) for h in range(heads)]
    below = [dot_pairs(pairs[2 * h + 1], split2(inner[h])) for h in range(heads)]
    for h in range(heads):
        _, beta_row, grow_row, inv_row, tail, decay, c_row, g3 = pre[h]
        top = []
        bottom = []
        for which, data in ((0, keys[h]), (1, values[h])):
            scale = [beta_row[:, a * W : a * W + W] for a in range(2)]
            if which == 0:
                scale = [
                    scale[a] * grow_row[:, a * W : a * W + W] * inv_row[a] for a in range(2)
                ]
            t00 = split2(times_rows(inverse[2 * h], scale[0]))
            t10 = split2(times_rows(below[h], -scale[0]))
            t11 = split2(times_rows(inverse[2 * h + 1], scale[1]))
            d0, d1 = data[:W], data[W:]
            top.append(
                mm(jnp.concatenate(t00, axis=1), jnp.concatenate([d0, d0], axis=0))
            )
            bottom.append(
                mm(
                    jnp.concatenate([t10[0], t11[0], t10[1], t11[1]], axis=1),
                    jnp.concatenate([d0, d1, d0, d1], axis=0),
                )
            )
        write = jnp.concatenate(
            [jnp.concatenate(top, axis=1), jnp.concatenate(bottom, axis=1)], axis=0
        )
        turned = keys[h].astype(F32).T.astype(BF16)
        weighted = split2(jnp.concatenate([tail, tail], axis=1) * write)
        both = mm(jnp.concatenate([turned, turned], axis=1), jnp.concatenate(weighted, axis=0))
        move = jnp.where(row == col, decay, 0.0) - both[:, :W]
        out.append((move, both[:, W:], write, c_row, inv_row, g3))
    return out


def local_reads(query, key, gate, write, c_row, inv_rows):
    g3 = jnp.concatenate(split3(jnp.broadcast_to(gate, (W, W))), axis=1)
    row = iota((W, W), 0)
    col = iota((W, W), 1)
    upto = bits(col <= row)
    c_tok = mm_nt(jnp.concatenate([upto] * 3, axis=1), g3)
    seen = mm_nt(query, key)
    weights = []
    for a in range(2):
        cols = slice(a * W, a * W + W)
        diff = minus_rows(c_tok, c_row[:, cols])
        ratio = jnp.exp(jnp.where(col + a * W <= 2 * row + 1, diff, -1e30))
        weights.append(ratio * times_rows(seen[:, cols], inv_rows[:, cols]))
    both = dot_pairs(split2(jnp.concatenate(weights, axis=1)), write)
    return jnp.exp(c_tok) * query.astype(F32) - both[:, :W], both[:, W:]


def apply(left, right):
    if left[1] is None and right[1] is None:
        return mm(left[0], right[0])
    if left[1] is None:
        return mm(
            jnp.concatenate([left[0], left[0]], axis=1), jnp.concatenate(right, axis=0)
        )
    if right[1] is None:
        return dot_pair_one(left, right[0])
    return dot_pairs(left, right)


def compose(later, earlier):
    move = apply(later[0], earlier[0])
    offset = apply(later[0], split2(earlier[1])) + later[1]
    return split2(move), offset


def kernel(
    n_y,
    n_tp,
    q_hbm,
    k_hbm,
    v_hbm,
    beta_hbm,
    gate_hbm,
    gain_hbm,
    w_ref,
    o_ref,
    k_buf,
    v_buf,
    q_ref,
    beta_ref,
    gate_ref,
    gain_ref,
    written,
    rows_buf,
    w_buf,
    y_send,
    y_recv,
    l_send,
    l_recv,
    h_send,
    h_recv,
    pre_m,
    pre_n,
    state,
    r_send,
    r_recv,
    n_send,
    n_buf,
    w_ssem,
    w_rsem,
    w_lsem,
    y_ssem,
    y_rsem,
    l_ssem,
    l_rsem,
    h_ssem,
    h_rsem,
    r_ssem,
    r_rsem,
    n_ssem,
    n_rsem,
    f_ssem,
    i_sem,
    u_ssem,
    u_rsem,
    ready,
):
    ctx = lax.axis_index("ctx")
    tp = lax.axis_index("tp")
    y = lax.rem(ctx, n_y)
    z = ctx // n_y
    zl = lax.rem(z, 4)
    zg = z // 4
    core = lax.rem(tp, 2)
    wide = 512

    def at(zz, yy):
        return zz * n_y + yy

    loads = []
    for i, (ref, buf) in enumerate(((k_hbm, k_buf), (v_hbm, v_buf))):
        for h in range(2):
            copy = pltpu.make_async_copy(
                ref.reshape(2 * W, 2 * W).at[:, pl.ds(h * W, W)], buf.at[h], i_sem.at[2 * i + h]
            )
            copy.start()
            loads.append(copy)

    for i, (ref, buf) in enumerate(
        ((beta_hbm, beta_ref), (gate_hbm, gate_ref), (q_hbm, q_ref), (gain_hbm, gain_ref))
    ):
        copy = pltpu.make_async_copy(ref, buf, i_sem.at[4 + i])
        copy.start()
        loads.append(copy)

    barrier = pltpu.get_barrier_semaphore()
    near = [(ctx, lax.rem(tp + d, n_tp)) for d in range(1, n_tp)]
    near += [
        (at(z, lax.rem(y + d, n_y)), lax.rem(tp + 2 * e, n_tp)) for d in range(1, n_y) for e in range(4)
    ]
    near += [(at(zg * 4 + lax.rem(zl + d, 4), y), tp) for d in range(1, 4)]
    for peer in near:
        pl.semaphore_signal(barrier, inc=1, device_id=peer, device_id_type=MESH)
    for d in range(1, 4):

        @pl.when(zg + d < 4)
        def _():
            pl.semaphore_signal(
                barrier, inc=1, device_id=(at(lax.rem(z + 4 * d, 16), y), tp), device_id_type=MESH
            )

    masks = make_masks()
    for copy in loads:
        copy.wait()
    keys = [k_buf[h] for h in range(2)]
    values = [v_buf[h] for h in range(2)]
    beta0 = [beta_ref[h : h + 1, :] for h in range(2)]
    beta1 = [beta_ref[2 + h : 3 + h, :] for h in range(2)]
    gates = [gate_ref[h : h + 1, :] for h in range(2)]

    def y_copy(j):
        owner = 2 * core + j
        return pltpu.make_async_remote_copy(
            y_send.at[j], y_recv.at[y], y_ssem.at[j], y_rsem.at[y], (at(z, owner), tp), MESH
        )

    def r_copy(j):
        owner = 2 * core + j
        return pltpu.make_async_remote_copy(
            r_send.at[j], r_recv.at[y], r_ssem.at[j], r_rsem.at[y], (at(z, owner), tp), MESH
        )

    @pl.when(tp >= 0)
    def _():
        made = local_maps(masks, keys, values, beta0, beta1, gates)
        for j in range(2):
            move = made[j][0].astype(BF16)
            offset = made[j][1].astype(BF16)
            hi, lo = split2(made[j][2])
            written[j, 0] = hi
            written[j, 1] = lo
            rows_buf[j, 0] = made[j][3]
            rows_buf[j, 1] = jnp.concatenate(made[j][4], axis=1)

            @pl.when(y == 2 * core + j)
            def _():
                y_recv[y, 0] = move
                y_recv[y, 1] = offset

            @pl.when(y != 2 * core + j)
            def _():
                y_send[j, 0] = move
                y_send[j, 1] = offset

    pl.semaphore_wait(barrier, len(near) + zg)
    for d in range(1, 4):

        @pl.when(zg - d >= 0)
        def _():
            pl.semaphore_signal(
                ready, inc=1, device_id=(at(lax.rem(z + 16 - 4 * d, 16), y), tp),
                device_id_type=MESH,
            )

    for j in range(2):

        @pl.when(y != 2 * core + j)
        def _():
            y_copy(j).start()

    def w_columns(owner):
        return w_ref.at[:, pl.ds(pl.multiple_of(owner * wide, wide), wide)]

    side = lax.rem(y, 2)
    chip = tp // 2
    partner = chip * 2 + 1 - core

    def w_copy(d, flip):
        owner = lax.rem(chip + d, 4) * 2 + lax.rem(core + flip, 2)
        return pltpu.make_async_remote_copy(
            w_columns(owner), w_buf.at[tp], w_ssem.at[2 * d + flip], w_rsem.at[tp],
            (ctx, owner), MESH,
        )

    w_far = ((1, 0), (3, 0), (1, 1), (3, 1), (2, 0), (2, 1))

    @pl.when(core == side)
    def _():
        for d, flip in w_far:
            w_copy(d, flip).start()

    w_copy(0, 1).start()
    w_own = pltpu.make_async_copy(w_columns(tp), w_buf.at[tp], w_lsem)
    w_own.start()

    def w_half(d, k):
        x = lax.rem(chip + d, 4)
        half = w_buf.at[x * 2 + side, pl.ds(k * W, W)]
        return pltpu.make_async_remote_copy(
            half, half, u_ssem.at[2 * d + k], u_rsem.at[2 * x + k],
            (at(z, lax.rem(y + (1 if k == 0 else n_y - 1), n_y)), tp), MESH,
        )

    def w_share(d):
        src = lax.rem(chip + d, 4) * 2 + side
        pltpu.make_async_remote_copy(
            w_buf.at[src], w_buf.at[src], w_ssem.at[0], w_rsem.at[src], (ctx, partner), MESH
        ).wait_recv()
        for k in range(2):
            w_half(d, k).start()

    def w_shared(d, k):
        x = lax.rem(chip + d, 4)
        half = w_buf.at[x * 2 + 1 - side, pl.ds(k * W, W)]
        pltpu.make_async_remote_copy(
            half, half, u_ssem.at[0], u_rsem.at[2 * x + k], (ctx, partner), MESH
        ).wait_recv()

    @pl.when(tp >= 0)
    def _():
        for j in range(2):
            eff, loc = local_reads(
                q_ref[:, j * W : j * W + W], k_buf[j], gate_ref[j : j + 1, :],
                (written[j, 0], written[j, 1]), rows_buf[j, 0], rows_buf[j, 1],
            )
            eff = eff.astype(BF16)
            loc = loc.astype(BF16)

            @pl.when(y == 2 * core + j)
            def _():
                r_recv[y, 0] = eff
                r_recv[y, 1] = loc

            @pl.when(y != 2 * core + j)
            def _():
                r_send[j, 0] = eff
                r_send[j, 1] = loc
                r_copy(j).start()

    def l_copy(d):
        other = lax.rem(zl + d, 4)
        return pltpu.make_async_remote_copy(
            l_send, l_recv.at[zl], l_ssem.at[d], l_rsem.at[zl], (at(zg * 4 + other, y), tp), MESH
        )

    def h_copy(d):
        return pltpu.make_async_remote_copy(
            h_send, h_recv.at[zg], h_ssem.at[d], h_rsem.at[zg],
            (at(lax.rem(z + 4 * d, 16), y), tp), MESH,
        )

    def h_copy_first(d):
        return pltpu.make_async_remote_copy(
            h_send.at[1], h_recv.at[0, 1], h_ssem.at[d], h_rsem.at[0],
            (at(lax.rem(z + 4 * d, 16), y), tp), MESH,
        )

    def n_copy(dy, dx):
        s = lax.rem(y + dy, n_y)
        other = lax.rem(chip + dx, 4) * 2 + core
        return pltpu.make_async_remote_copy(
            n_send.at[s], n_buf.at[chip * 4 + y], n_ssem.at[dy * 4 + dx],
            n_rsem.at[chip * 4 + y], (at(z, s), other), MESH,
        )

    def ready_wait():
        @pl.when(zg < 3)
        def _():
            pl.semaphore_wait(ready, 3 - zg)

    @pl.when(y // 2 != core)
    def _():
        for d in (1, 3, 2):
            w_share(d)
        ready_wait()

    @pl.when(y // 2 == core)
    def _():
        for s in range(n_y):

            @pl.when(s != y)
            def _():
                pltpu.make_async_remote_copy(
                    y_recv.at[s], y_recv.at[s], y_ssem.at[0], y_rsem.at[s],
                    (at(z, s), tp), MESH,
                ).wait_recv()

        part = [
            ((y_recv[s, 0], None), y_recv[s, 1].astype(F32)) for s in range(n_y)
        ]
        first_two = compose(part[1], part[0])
        last_two = compose(part[3], part[2])
        whole = compose(last_two, first_two)
        l_send[0] = whole[0][0]
        l_send[1] = whole[1].astype(BF16)
        for d in (3, 1, 2):
            l_copy(d).start()
        l_recv[zl, 0] = whole[0][0]
        l_recv[zl, 1] = whole[1].astype(BF16)
        for d in range(1, 4):
            src = lax.rem(zl + d, 4)
            pltpu.make_async_remote_copy(
                l_recv.at[src], l_recv.at[src], l_ssem.at[d], l_rsem.at[src],
                (at(zg * 4 + src, y), tp), MESH,
            ).wait_recv()
        grp = [((l_recv[s, 0], None), l_recv[s, 1].astype(F32)) for s in range(4)]
        low_two = compose(grp[1], grp[0])
        high_two = compose(grp[3], grp[2])
        total = compose(high_two, low_two)
        h_send[0] = total[0][0]
        h_send[1] = total[1].astype(BF16)
        ready_wait()
        @pl.when(zg == 0)
        def _():
            for d in (2, 3, 1):
                h_copy_first(d).start()

        for d in (2, 1):

            @pl.when((zg > 0) & (zg + d < 4))
            def _():
                h_copy(d).start()

        w_share(1)
        w_share(3)

        @pl.when(tp >= 0)
        def _():
            row = iota((W, W), 0)
            col = iota((W, W), 1)
            eye = (row == col).astype(F32)
            three = compose(part[2], first_two)
            low_three = compose(grp[2], low_two)

            def joined(pair):
                return pair[0].astype(F32) + pair[1].astype(F32)

            entry_m = jnp.where(
                zl == 0,
                eye,
                jnp.where(
                    zl == 1,
                    grp[0][0][0].astype(F32),
                    jnp.where(zl == 2, joined(low_two[0]), joined(low_three[0])),
                ),
            )
            entry_n = jnp.where(
                zl == 0,
                0.0,
                jnp.where(zl == 1, grp[0][1], jnp.where(zl == 2, low_two[1], low_three[1])),
            )
            entry = (split2(entry_m), entry_n)
            starts = [entry] + [compose(p, entry) for p in (part[0], first_two, three)]
            for s in range(n_y):

                @pl.when(s != y)
                def _():
                    pltpu.make_async_remote_copy(
                        r_recv.at[s], r_recv.at[s], r_ssem.at[0], r_rsem.at[s],
                        (at(z, s), tp), MESH,
                    ).wait_recv()

            for s in range(n_y):
                read = r_recv[s, 0]
                twice = jnp.concatenate([read, read], axis=1)
                move = split2(mm(twice, jnp.concatenate(starts[s][0], axis=0)))
                pre_m[s] = left3(move)
                pre_n[s] = mm(
                    twice, jnp.concatenate(split2(starts[s][1]), axis=0)
                ) + r_recv[s, 1].astype(F32)
            state[...] = jnp.zeros((W, W), F32)

        w_share(2)
        for s in range(3):

            @pl.when(s < zg)
            def _():
                if s == 0:
                    pltpu.make_async_remote_copy(
                        h_recv.at[0, 1], h_recv.at[0, 1], h_ssem.at[0], h_rsem.at[0],
                        (at(z, y), tp), MESH,
                    ).wait_recv()
                    state[...] = h_recv[0, 1].astype(F32)
                else:
                    pltpu.make_async_remote_copy(
                        h_recv.at[s], h_recv.at[s], h_ssem.at[0], h_rsem.at[s],
                        (at(z, y), tp), MESH,
                    ).wait_recv()
                    now = split2(state[...])
                    state[...] = mm(
                        jnp.concatenate([h_recv[s, 0], h_recv[s, 0]], axis=1),
                        jnp.concatenate([now[0], now[1]], axis=0),
                    ) + h_recv[s, 1].astype(F32)

        entering = right3(split2(state[...]))
        gain = jnp.where(
            lax.rem(y, 2) == 0, gain_ref[:, :W], gain_ref[:, W:]
        )
        for dy in (2, 1, 3, 0):
            s = lax.rem(y + dy, n_y)
            out = mm(pre_m[s], entering) + pre_n[s]
            scale = lax.rsqrt(jnp.mean(out * out, axis=1, keepdims=True) + 1e-06)
            done = (out * scale * gain).astype(BF16)
            n_send[s] = done
            if dy == 0:
                n_buf[chip * 4 + y] = done
            for dx in (2, 1, 3, 0):
                if dx or dy:
                    n_copy(dy, dx).start()

    def pass_on(j, dx):
        head = lax.rem(chip + dx, 4) * 4 + 2 * core + j
        return pltpu.make_async_remote_copy(
            n_buf.at[head], n_buf.at[head], f_ssem.at[j * 4 + dx], n_rsem.at[head],
            (ctx, partner), MESH,
        )

    def arrived(head):
        pltpu.make_async_remote_copy(
            n_buf.at[head], n_buf.at[head], f_ssem.at[0], n_rsem.at[head], (ctx, partner), MESH
        ).wait_recv()

    def w_ready(dx, of):
        @pl.when(of != side)
        def _():
            for k in range(2):
                w_shared(dx, k)

    def term(first, src):
        both = jnp.concatenate([n_buf[first], n_buf[first + 1]], axis=1)
        return mm(both, w_buf[src])

    total = None
    for dx in (0, 1, 3, 2):
        src = lax.rem(chip + dx, 4) * 2 + core
        first = lax.rem(chip + dx, 4) * 4 + 2 * core
        for j in range(2):
            if dx == 0:

                @pl.when(y != 2 * core + j)
                def _():
                    arrived(first + j)

            else:
                arrived(first + j)
            pass_on(j, dx).start()
        if dx == 0:
            w_own.wait()
        else:
            w_ready(dx, core)
        part = term(first, src)
        total = part if total is None else total + part
    for dx in (0, 1, 3, 2):
        src = lax.rem(chip + dx, 4) * 2 + 1 - core
        first = lax.rem(chip + dx, 4) * 4 + 2 * (1 - core)
        if dx == 0:
            pltpu.make_async_remote_copy(
                w_buf.at[partner], w_buf.at[partner], w_ssem.at[0], w_rsem.at[partner],
                (ctx, partner), MESH,
            ).wait_recv()
        else:
            w_ready(dx, 1 - core)
        arrived(first)
        arrived(first + 1)
        total = total + term(first, src)
    o_ref[...] = total.astype(BF16)

    w_copy(0, 1).wait_send()

    @pl.when(core == side)
    def _():
        for d, flip in w_far:
            w_copy(d, flip).wait_send()

    for d in range(1, 4):
        for k in range(2):
            w_half(d, k).wait_send()

    for j in range(2):
        for dx in range(4):
            pass_on(j, dx).wait_send()

        @pl.when(y != 2 * core + j)
        def _():
            y_copy(j).wait_send()
            r_copy(j).wait_send()

    @pl.when(y // 2 == core)
    def _():
        for d in range(1, 4):
            l_copy(d).wait_send()

            @pl.when(zg == 0)
            def _():
                h_copy_first(d).wait_send()

            @pl.when((zg > 0) & (zg + d < 4))
            def _():
                h_copy(d).wait_send()

        for dy in range(n_y):
            for dx in range(4):
                if dx or dy:
                    n_copy(dy, dx).wait_send()


def local(queries, key_vectors, value_vectors, strengths, log_gate, out_gain, out_weight):
    tokens = queries.shape[0]
    n_tp = 8
    n_y = 4
    width = out_weight.shape[1] // n_tp
    vmem = pl.BlockSpec(memory_space=pltpu.VMEM)
    hbm = pl.BlockSpec(memory_space=pl.ANY)
    dma = pltpu.SemaphoreType.DMA
    return pl.pallas_call(
        functools.partial(kernel, n_y, n_tp),
        out_shape=jax.ShapeDtypeStruct((tokens, width), BF16),
        in_specs=[hbm] * 7,
        out_specs=vmem,
        scratch_shapes=[
            pltpu.VMEM((2, 2 * W, W), BF16),
            pltpu.VMEM((2, 2 * W, W), BF16),
            pltpu.VMEM((W, 2 * W), BF16),
            pltpu.VMEM((4, W), F32),
            pltpu.VMEM((2, W), F32),
            pltpu.VMEM((1, 2 * W), F32),
            pltpu.VMEM((2, 2, 2 * W, 2 * W), BF16),
            pltpu.VMEM((2, 2, 8, 2 * W), F32),
            pltpu.VMEM((n_tp, 2 * W, width), BF16),
            pltpu.VMEM((2, 2, W, W), BF16),
            pltpu.VMEM((n_y, 2, W, W), BF16),
            pltpu.VMEM((2, W, W), BF16),
            pltpu.VMEM((4, 2, W, W), BF16),
            pltpu.VMEM((2, W, W), BF16),
            pltpu.VMEM((4, 2, W, W), BF16),
            pltpu.VMEM((n_y, W, 3 * W), BF16),
            pltpu.VMEM((n_y, W, W), F32),
            pltpu.VMEM((W, W), F32),
            pltpu.VMEM((2, 2, W, W), BF16),
            pltpu.VMEM((n_y, 2, W, W), BF16),
            pltpu.VMEM((n_y, W, W), BF16),
            pltpu.VMEM((2 * n_tp, W, W), BF16),
            dma((n_tp,)),
            dma((n_tp,)),
            dma,
            dma((2,)),
            dma((n_y,)),
            dma((4,)),
            dma((4,)),
            dma((4,)),
            dma((4,)),
            dma((2,)),
            dma((n_y,)),
            dma((16,)),
            dma((16,)),
            dma((8,)),
            dma((8,)),
            dma((8,)),
            dma((8,)),
            pltpu.SemaphoreType.REGULAR,
        ],
        compiler_params=pltpu.CompilerParams(collective_id=0, has_side_effects=True),
    )(
        queries,
        key_vectors,
        value_vectors,
        strengths.reshape(4, tokens),
        log_gate,
        out_gain.reshape(1, -1),
        out_weight,
    )


def solution(mesh):
    placed = (
        P("ctx", "tp"),
        P("ctx", None, "tp"),
        P("ctx", None, "tp"),
        P(None, "tp", "ctx"),
        P("tp", "ctx"),
        P("tp"),
        P("tp", None),
    )
    return jax.shard_map(
        local, mesh=mesh, in_specs=placed, out_specs=P("ctx", "tp"), check_vma=False
    )
```

```python
import functools

import jax
import jax.numpy as jnp
from jax import lax
from jax.experimental import pallas as pl
from jax.experimental.pallas import tpu as pltpu
from jax.sharding import PartitionSpec as P

MESH = pl.DeviceIdType.MESH
F32 = jnp.float32
BF16 = jnp.bfloat16
W = 128


def mm(a, b):
    return jnp.dot(a, b, preferred_element_type=F32)


def mm_nt(a, b):
    return lax.dot_general(a, b, (((1,), (1,)), ((), ())), preferred_element_type=F32)


def split2(a):
    hi = a.astype(BF16)
    return hi, (a - hi.astype(F32)).astype(BF16)


def split3(a):
    hi = a.astype(BF16)
    rest = a - hi.astype(F32)
    mid = rest.astype(BF16)
    return hi, mid, (rest - mid.astype(F32)).astype(BF16)


def left3(pair):
    return jnp.concatenate([pair[0], pair[1], pair[0]], axis=1)


def right3(pair):
    return jnp.concatenate([pair[0], pair[0], pair[1]], axis=0)


def dot_pairs(a, b):
    return mm(left3(a), right3(b))


def dot_pair_one(a, b):
    return mm(jnp.concatenate([a[0], a[1]], axis=1), jnp.concatenate([b, b], axis=0))


def x3(a, b):
    return dot_pairs(split2(a), split2(b))


def iota(shape, dim):
    return lax.broadcasted_iota(jnp.int32, shape, dim)


def bits(mask):
    return mask.astype(F32).astype(BF16)


def by_rows(block, rows):
    n = block.shape[0]
    return block.reshape(n // 8, 8, W), jnp.broadcast_to(rows[None], (n // 8, 8, W))


def times_rows(block, rows):
    a, b = by_rows(block, rows)
    return (a * b).reshape(block.shape)


def minus_rows(block, rows):
    a, b = by_rows(block, rows)
    return (a - b).reshape(block.shape)


def make_masks():
    step = iota((2 * W, W), 0)
    token = iota((2 * W, W), 1)
    row = iota((W, W), 0)
    col = iota((W, W), 1)
    upto = bits(2 * token <= step)
    first = bits(2 * token == step)
    second = bits(2 * token + 1 == step)
    levels = []
    size = 1
    while size < W:
        levels.append(bits((row // size == col // size + 1) & ((row // size) % 2 == 1)))
        size *= 2
    return (
        jnp.concatenate([upto] * 3, axis=1),
        jnp.concatenate([first] * 3 + [second] * 3, axis=1),
        levels,
    )


def local_maps(masks, keys, values, beta0, beta1, gate):
    heads = len(keys)
    upto3, pick, levels = masks
    row = iota((W, W), 0)
    col = iota((W, W), 1)
    eye = (row == col).astype(F32)
    pre = []
    low = []
    for h in range(heads):
        k = keys[h]
        k32 = k.astype(F32)
        gram = mm_nt(k, k)
        inv_col = lax.rsqrt(jnp.sum(k32 * k32, axis=1, keepdims=True) + 1e-06)
        inv_row = []
        for a in range(2):
            part = jnp.where(row == col, gram[a * W : a * W + W, a * W : a * W + W], 0.0)
            total = jnp.sum(part.reshape(W // 8, 8, W), axis=0)
            total = jnp.broadcast_to(jnp.sum(total, axis=0, keepdims=True), (8, W))
            inv_row.append(lax.rsqrt(total + 1e-06))
        g3 = jnp.concatenate(split3(jnp.broadcast_to(gate[h], (W, W))), axis=1)
        b3 = jnp.concatenate(
            split3(jnp.broadcast_to(beta0[h], (W, W))) + split3(jnp.broadcast_to(beta1[h], (W, W))),
            axis=1,
        )
        c_col = mm_nt(upto3, g3)
        c_row = mm_nt(g3[:8], upto3)
        beta = mm_nt(pick, b3)
        beta_row = mm_nt(b3[:8], pick)
        grow_row = jnp.exp(c_row)
        scaled = beta * inv_col
        blocks = {}
        for a, b in ((0, 0), (1, 1), (1, 0)):
            ra, cb = slice(a * W, a * W + W), slice(b * W, b * W + W)
            diff = minus_rows(c_col[ra], c_row[:, cb])
            if a == b:
                diff = jnp.where(row > col, diff, -1e30)
            block = scaled[ra] * jnp.exp(diff) * times_rows(gram[ra, cb], inv_row[b])
            blocks[a, b] = split2(block)
        last = c_col[2 * W - 1 : 2 * W]
        tail = inv_col * jnp.exp(last - c_col)
        pre.append((blocks[1, 0], beta_row, grow_row, inv_row, tail, jnp.exp(last), c_row, g3))
        low += [blocks[0, 0], blocks[1, 1]]
    inverse = [
        eye - (part[0] * levels[0]).astype(F32) - (part[1] * levels[0]).astype(F32) for part in low
    ]
    for mask in levels[1:]:
        pairs = [split2(t) for t in inverse]
        inner = [
            dot_pairs((part[0] * mask, part[1] * mask), pair) for part, pair in zip(low, pairs)
        ]
        inverse = [t - dot_pairs(pair, split2(c)) for t, pair, c in zip(inverse, pairs, inner)]
    out = []
    pairs = [split2(t) for t in inverse]
    inner = [dot_pairs(pre[h][0], pairs[2 * h]) for h in range(heads)]
    below = [dot_pairs(pairs[2 * h + 1], split2(inner[h])) for h in range(heads)]
    for h in range(heads):
        _, beta_row, grow_row, inv_row, tail, decay, c_row, g3 = pre[h]
        top = []
        bottom = []
        for which, data in ((0, keys[h]), (1, values[h])):
            scale = [beta_row[:, a * W : a * W + W] for a in range(2)]
            if which == 0:
                scale = [
                    scale[a] * grow_row[:, a * W : a * W + W] * inv_row[a] for a in range(2)
                ]
            t00 = split2(times_rows(inverse[2 * h], scale[0]))
            t10 = split2(times_rows(below[h], -scale[0]))
            t11 = split2(times_rows(inverse[2 * h + 1], scale[1]))
            d0, d1 = data[:W], data[W:]
            top.append(
                mm(jnp.concatenate(t00, axis=1), jnp.concatenate([d0, d0], axis=0))
            )
            bottom.append(
                mm(
                    jnp.concatenate([t10[0], t11[0], t10[1], t11[1]], axis=1),
                    jnp.concatenate([d0, d1, d0, d1], axis=0),
                )
            )
        write = jnp.concatenate(
            [jnp.concatenate(top, axis=1), jnp.concatenate(bottom, axis=1)], axis=0
        )
        turned = keys[h].astype(F32).T.astype(BF16)
        weighted = split2(jnp.concatenate([tail, tail], axis=1) * write)
        both = mm(jnp.concatenate([turned, turned], axis=1), jnp.concatenate(weighted, axis=0))
        move = jnp.where(row == col, decay, 0.0) - both[:, :W]
        out.append((move, both[:, W:], write, c_row, inv_row, g3))
    return out


def local_reads(query, key, gate, write, c_row, inv_rows):
    g3 = jnp.concatenate(split3(jnp.broadcast_to(gate, (W, W))), axis=1)
    row = iota((W, W), 0)
    col = iota((W, W), 1)
    upto = bits(col <= row)
    c_tok = mm_nt(jnp.concatenate([upto] * 3, axis=1), g3)
    seen = mm_nt(query, key)
    weights = []
    for a in range(2):
        cols = slice(a * W, a * W + W)
        diff = minus_rows(c_tok, c_row[:, cols])
        ratio = jnp.exp(jnp.where(col + a * W <= 2 * row + 1, diff, -1e30))
        weights.append(ratio * times_rows(seen[:, cols], inv_rows[:, cols]))
    both = dot_pairs(split2(jnp.concatenate(weights, axis=1)), write)
    return jnp.exp(c_tok) * query.astype(F32) - both[:, :W], both[:, W:]


def apply(left, right):
    if left[1] is None and right[1] is None:
        return mm(left[0], right[0])
    if left[1] is None:
        return mm(
            jnp.concatenate([left[0], left[0]], axis=1), jnp.concatenate(right, axis=0)
        )
    if right[1] is None:
        return dot_pair_one(left, right[0])
    return dot_pairs(left, right)


def compose(later, earlier):
    move = apply(later[0], earlier[0])
    offset = apply(later[0], split2(earlier[1])) + later[1]
    return split2(move), offset


def kernel(
    n_y,
    n_tp,
    q_hbm,
    k_hbm,
    v_hbm,
    beta_hbm,
    gate_hbm,
    gain_hbm,
    w_ref,
    o_ref,
    k_buf,
    v_buf,
    q_ref,
    beta_ref,
    gate_ref,
    gain_ref,
    written,
    rows_buf,
    w_buf,
    y_send,
    y_recv,
    l_send,
    l_recv,
    h_send,
    h_recv,
    pre_m,
    pre_n,
    state,
    r_send,
    r_recv,
    n_send,
    n_buf,
    w_ssem,
    w_rsem,
    w_lsem,
    y_ssem,
    y_rsem,
    l_ssem,
    l_rsem,
    h_ssem,
    h_rsem,
    r_ssem,
    r_rsem,
    n_ssem,
    n_rsem,
    f_ssem,
    i_sem,
    u_ssem,
    u_rsem,
    ready,
):
    ctx = lax.axis_index("ctx")
    tp = lax.axis_index("tp")
    y = lax.rem(ctx, n_y)
    z = ctx // n_y
    zl = lax.rem(z, 4)
    zg = z // 4
    core = lax.rem(tp, 2)
    wide = 512

    def at(zz, yy):
        return zz * n_y + yy

    loads = []
    for i, (ref, buf) in enumerate(((k_hbm, k_buf), (v_hbm, v_buf))):
        for h in range(2):
            copy = pltpu.make_async_copy(
                ref.reshape(2 * W, 2 * W).at[:, pl.ds(h * W, W)], buf.at[h], i_sem.at[2 * i + h]
            )
            copy.start()
            loads.append(copy)

    for i, (ref, buf) in enumerate(
        ((beta_hbm, beta_ref), (gate_hbm, gate_ref), (q_hbm, q_ref), (gain_hbm, gain_ref))
    ):
        copy = pltpu.make_async_copy(ref, buf, i_sem.at[4 + i])
        copy.start()
        loads.append(copy)

    barrier = pltpu.get_barrier_semaphore()
    near = [(ctx, lax.rem(tp + d, n_tp)) for d in range(1, n_tp)]
    near += [
        (at(z, lax.rem(y + d, n_y)), lax.rem(tp + 2 * e, n_tp)) for d in range(1, n_y) for e in range(4)
    ]
    near += [(at(zg * 4 + lax.rem(zl + d, 4), y), tp) for d in range(1, 4)]
    for peer in near:
        pl.semaphore_signal(barrier, inc=1, device_id=peer, device_id_type=MESH)
    for d in range(1, 4):

        @pl.when(zg + d < 4)
        def _():
            pl.semaphore_signal(
                barrier, inc=1, device_id=(at(lax.rem(z + 4 * d, 16), y), tp), device_id_type=MESH
            )

    masks = make_masks()
    for copy in loads:
        copy.wait()
    keys = [k_buf[h] for h in range(2)]
    values = [v_buf[h] for h in range(2)]
    beta0 = [beta_ref[h : h + 1, :] for h in range(2)]
    beta1 = [beta_ref[2 + h : 3 + h, :] for h in range(2)]
    gates = [gate_ref[h : h + 1, :] for h in range(2)]

    def y_copy(j):
        owner = 2 * core + j
        return pltpu.make_async_remote_copy(
            y_send.at[j], y_recv.at[y], y_ssem.at[j], y_rsem.at[y], (at(z, owner), tp), MESH
        )

    def r_copy(j):
        owner = 2 * core + j
        return pltpu.make_async_remote_copy(
            r_send.at[j], r_recv.at[y], r_ssem.at[j], r_rsem.at[y], (at(z, owner), tp), MESH
        )

    @pl.when(tp >= 0)
    def _():
        made = local_maps(masks, keys, values, beta0, beta1, gates)
        for j in range(2):
            move = made[j][0].astype(BF16)
            offset = made[j][1].astype(BF16)
            hi, lo = split2(made[j][2])
            written[j, 0] = hi
            written[j, 1] = lo
            rows_buf[j, 0] = made[j][3]
            rows_buf[j, 1] = jnp.concatenate(made[j][4], axis=1)

            @pl.when(y == 2 * core + j)
            def _():
                y_recv[y, 0] = move
                y_recv[y, 1] = offset

            @pl.when(y != 2 * core + j)
            def _():
                y_send[j, 0] = move
                y_send[j, 1] = offset

    pl.semaphore_wait(barrier, len(near) + zg)
    for d in range(1, 4):

        @pl.when(zg - d >= 0)
        def _():
            pl.semaphore_signal(
                ready, inc=1, device_id=(at(lax.rem(z + 16 - 4 * d, 16), y), tp),
                device_id_type=MESH,
            )

    for j in range(2):

        @pl.when(y != 2 * core + j)
        def _():
            y_copy(j).start()

    def w_columns(owner):
        return w_ref.at[:, pl.ds(pl.multiple_of(owner * wide, wide), wide)]

    side = lax.rem(y, 2)
    chip = tp // 2
    partner = chip * 2 + 1 - core

    def w_copy(d, flip):
        owner = lax.rem(chip + d, 4) * 2 + lax.rem(core + flip, 2)
        rows = pl.ds(pl.multiple_of(side * W, W), W)
        columns = pl.ds(pl.multiple_of(owner * wide, wide), wide)
        return pltpu.make_async_remote_copy(
            w_ref.at[rows, columns], w_buf.at[tp, rows], w_ssem.at[2 * d + flip], w_rsem.at[tp],
            (ctx, owner), MESH,
        )

    w_far = ((1, 0), (3, 0), (1, 1), (3, 1), (2, 0), (2, 1))
    for d, flip in w_far:
        w_copy(d, flip).start()
    w_near = pltpu.make_async_remote_copy(
        w_columns(partner), w_buf.at[tp], w_ssem.at[1], w_rsem.at[tp], (ctx, partner), MESH
    )
    w_near.start()
    w_own = pltpu.make_async_copy(w_columns(tp), w_buf.at[tp], w_lsem)
    w_own.start()

    def w_quarter(d, c, k):
        x = lax.rem(chip + d, 4)
        part = w_buf.at[x * 2 + c, pl.ds(pl.multiple_of(side * W + k * (W // 2), W // 2), W // 2)]
        return pltpu.make_async_remote_copy(
            part, part, u_ssem.at[4 * d + 2 * c + k], u_rsem.at[4 * x + 2 * c + k],
            (at(z, lax.rem(y + (1 if k == 0 else n_y - 1), n_y)), tp), MESH,
        )

    def w_share(d):
        for c in range(2):
            src = lax.rem(chip + d, 4) * 2 + c
            part = w_buf.at[src, pl.ds(pl.multiple_of(side * W, W), W)]
            pltpu.make_async_remote_copy(
                part, part, w_ssem.at[0], w_rsem.at[src], (ctx, partner), MESH
            ).wait_recv()
            for k in range(2):
                w_quarter(d, c, k).start()

    def w_ready(d, c):
        x = lax.rem(chip + d, 4)
        for k in range(2):
            part = w_buf.at[
                x * 2 + c, pl.ds(pl.multiple_of((1 - side) * W + k * (W // 2), W // 2), W // 2)
            ]
            pltpu.make_async_remote_copy(
                part, part, u_ssem.at[0], u_rsem.at[4 * x + 2 * c + k], (ctx, partner), MESH
            ).wait_recv()

    @pl.when(tp >= 0)
    def _():
        for j in range(2):
            eff, loc = local_reads(
                q_ref[:, j * W : j * W + W], k_buf[j], gate_ref[j : j + 1, :],
                (written[j, 0], written[j, 1]), rows_buf[j, 0], rows_buf[j, 1],
            )
            eff = eff.astype(BF16)
            loc = loc.astype(BF16)

            @pl.when(y == 2 * core + j)
            def _():
                r_recv[y, 0] = eff
                r_recv[y, 1] = loc

            @pl.when(y != 2 * core + j)
            def _():
                r_send[j, 0] = eff
                r_send[j, 1] = loc
                r_copy(j).start()

    def l_copy(d):
        other = lax.rem(zl + d, 4)
        return pltpu.make_async_remote_copy(
            l_send, l_recv.at[zl], l_ssem.at[d], l_rsem.at[zl], (at(zg * 4 + other, y), tp), MESH
        )

    def h_copy(d):
        return pltpu.make_async_remote_copy(
            h_send, h_recv.at[zg], h_ssem.at[d], h_rsem.at[zg],
            (at(lax.rem(z + 4 * d, 16), y), tp), MESH,
        )

    def h_copy_first(d):
        return pltpu.make_async_remote_copy(
            h_send.at[1], h_recv.at[0, 1], h_ssem.at[d], h_rsem.at[0],
            (at(lax.rem(z + 4 * d, 16), y), tp), MESH,
        )

    def n_copy(dy, dx):
        s = lax.rem(y + dy, n_y)
        other = lax.rem(chip + dx, 4) * 2 + core
        return pltpu.make_async_remote_copy(
            n_send.at[s], n_buf.at[chip * 4 + y], n_ssem.at[dy * 4 + dx],
            n_rsem.at[chip * 4 + y], (at(z, s), other), MESH,
        )

    def ready_wait():
        @pl.when(zg < 3)
        def _():
            pl.semaphore_wait(ready, 3 - zg)

    @pl.when(y // 2 != core)
    def _():
        for d in (1, 3, 2):
            w_share(d)
        ready_wait()

    @pl.when(y // 2 == core)
    def _():
        for s in range(n_y):

            @pl.when(s != y)
            def _():
                pltpu.make_async_remote_copy(
                    y_recv.at[s], y_recv.at[s], y_ssem.at[0], y_rsem.at[s],
                    (at(z, s), tp), MESH,
                ).wait_recv()

        part = [
            ((y_recv[s, 0], None), y_recv[s, 1].astype(F32)) for s in range(n_y)
        ]
        first_two = compose(part[1], part[0])
        last_two = compose(part[3], part[2])
        whole = compose(last_two, first_two)
        l_send[0] = whole[0][0]
        l_send[1] = whole[1].astype(BF16)
        for d in (3, 1, 2):
            l_copy(d).start()
        l_recv[zl, 0] = whole[0][0]
        l_recv[zl, 1] = whole[1].astype(BF16)
        for d in (1, 2, 3):
            if d == 3:
                w_share(1)
                w_share(3)
            src = lax.rem(zl + d, 4)
            pltpu.make_async_remote_copy(
                l_recv.at[src], l_recv.at[src], l_ssem.at[d], l_rsem.at[src],
                (at(zg * 4 + src, y), tp), MESH,
            ).wait_recv()
        grp = [((l_recv[s, 0], None), l_recv[s, 1].astype(F32)) for s in range(4)]
        low_two = compose(grp[1], grp[0])
        high_two = compose(grp[3], grp[2])
        total = compose(high_two, low_two)
        h_send[0] = total[0][0]
        h_send[1] = total[1].astype(BF16)
        ready_wait()
        @pl.when(zg == 0)
        def _():
            for d in (2, 3, 1):
                h_copy_first(d).start()

        for d in (2, 1):

            @pl.when((zg > 0) & (zg + d < 4))
            def _():
                h_copy(d).start()

        @pl.when(tp >= 0)
        def _():
            row = iota((W, W), 0)
            col = iota((W, W), 1)
            eye = (row == col).astype(F32)
            three = compose(part[2], first_two)
            low_three = compose(grp[2], low_two)

            def joined(pair):
                return pair[0].astype(F32) + pair[1].astype(F32)

            entry_m = jnp.where(
                zl == 0,
                eye,
                jnp.where(
                    zl == 1,
                    grp[0][0][0].astype(F32),
                    jnp.where(zl == 2, joined(low_two[0]), joined(low_three[0])),
                ),
            )
            entry_n = jnp.where(
                zl == 0,
                0.0,
                jnp.where(zl == 1, grp[0][1], jnp.where(zl == 2, low_two[1], low_three[1])),
            )
            entry = (split2(entry_m), entry_n)
            starts = [entry] + [compose(p, entry) for p in (part[0], first_two, three)]
            for s in range(n_y):

                @pl.when(s != y)
                def _():
                    pltpu.make_async_remote_copy(
                        r_recv.at[s], r_recv.at[s], r_ssem.at[0], r_rsem.at[s],
                        (at(z, s), tp), MESH,
                    ).wait_recv()

            for s in range(n_y):
                read = r_recv[s, 0]
                twice = jnp.concatenate([read, read], axis=1)
                move = split2(mm(twice, jnp.concatenate(starts[s][0], axis=0)))
                pre_m[s] = left3(move)
                pre_n[s] = mm(
                    twice, jnp.concatenate(split2(starts[s][1]), axis=0)
                ) + r_recv[s, 1].astype(F32)
            state[...] = jnp.zeros((W, W), F32)

        w_share(2)
        for s in range(3):

            @pl.when(s < zg)
            def _():
                if s == 0:
                    pltpu.make_async_remote_copy(
                        h_recv.at[0, 1], h_recv.at[0, 1], h_ssem.at[0], h_rsem.at[0],
                        (at(z, y), tp), MESH,
                    ).wait_recv()
                    state[...] = h_recv[0, 1].astype(F32)
                else:
                    pltpu.make_async_remote_copy(
                        h_recv.at[s], h_recv.at[s], h_ssem.at[0], h_rsem.at[s],
                        (at(z, y), tp), MESH,
                    ).wait_recv()
                    now = split2(state[...])
                    state[...] = mm(
                        jnp.concatenate([h_recv[s, 0], h_recv[s, 0]], axis=1),
                        jnp.concatenate([now[0], now[1]], axis=0),
                    ) + h_recv[s, 1].astype(F32)

        entering = right3(split2(state[...]))
        gain = jnp.where(
            lax.rem(y, 2) == 0, gain_ref[:, :W], gain_ref[:, W:]
        )
        for dy in (2, 1, 3, 0):
            s = lax.rem(y + dy, n_y)
            out = mm(pre_m[s], entering) + pre_n[s]
            scale = lax.rsqrt(jnp.mean(out * out, axis=1, keepdims=True) + 1e-06)
            done = (out * scale * gain).astype(BF16)
            n_send[s] = done
            if dy == 0:
                n_buf[chip * 4 + y] = done
            for dx in (2, 1, 3, 0):
                if dx or dy:
                    n_copy(dy, dx).start()

    def pass_on(j, dx):
        head = lax.rem(chip + dx, 4) * 4 + 2 * core + j
        return pltpu.make_async_remote_copy(
            n_buf.at[head], n_buf.at[head], f_ssem.at[j * 4 + dx], n_rsem.at[head],
            (ctx, partner), MESH,
        )

    def arrived(head):
        pltpu.make_async_remote_copy(
            n_buf.at[head], n_buf.at[head], f_ssem.at[0], n_rsem.at[head], (ctx, partner), MESH
        ).wait_recv()

    def term(first, src):
        both = jnp.concatenate([n_buf[first], n_buf[first + 1]], axis=1)
        return mm(both, w_buf[src])

    total = None
    for dx in (0, 1, 3, 2):
        src = lax.rem(chip + dx, 4) * 2 + core
        first = lax.rem(chip + dx, 4) * 4 + 2 * core
        for j in range(2):
            if dx == 0:

                @pl.when(y != 2 * core + j)
                def _():
                    arrived(first + j)

            else:
                arrived(first + j)
            pass_on(j, dx).start()
        if dx == 0:
            w_own.wait()
        else:
            w_ready(dx, core)
        part = term(first, src)
        total = part if total is None else total + part
    for dx in (0, 1, 3, 2):
        src = lax.rem(chip + dx, 4) * 2 + 1 - core
        first = lax.rem(chip + dx, 4) * 4 + 2 * (1 - core)
        if dx == 0:
            pltpu.make_async_remote_copy(
                w_buf.at[partner], w_buf.at[partner], w_ssem.at[0], w_rsem.at[partner],
                (ctx, partner), MESH,
            ).wait_recv()
        else:
            w_ready(dx, 1 - core)
        arrived(first)
        arrived(first + 1)
        total = total + term(first, src)
    o_ref[...] = total.astype(BF16)

    w_near.wait_send()
    for d, flip in w_far:
        w_copy(d, flip).wait_send()
    for d in range(1, 4):
        for c in range(2):
            for k in range(2):
                w_quarter(d, c, k).wait_send()

    for j in range(2):
        for dx in range(4):
            pass_on(j, dx).wait_send()

        @pl.when(y != 2 * core + j)
        def _():
            y_copy(j).wait_send()
            r_copy(j).wait_send()

    @pl.when(y // 2 == core)
    def _():
        for d in range(1, 4):
            l_copy(d).wait_send()

            @pl.when(zg == 0)
            def _():
                h_copy_first(d).wait_send()

            @pl.when((zg > 0) & (zg + d < 4))
            def _():
                h_copy(d).wait_send()

        for dy in range(n_y):
            for dx in range(4):
                if dx or dy:
                    n_copy(dy, dx).wait_send()


def local(queries, key_vectors, value_vectors, strengths, log_gate, out_gain, out_weight):
    tokens = queries.shape[0]
    n_tp = 8
    n_y = 4
    width = out_weight.shape[1] // n_tp
    vmem = pl.BlockSpec(memory_space=pltpu.VMEM)
    hbm = pl.BlockSpec(memory_space=pl.ANY)
    dma = pltpu.SemaphoreType.DMA
    return pl.pallas_call(
        functools.partial(kernel, n_y, n_tp),
        out_shape=jax.ShapeDtypeStruct((tokens, width), BF16),
        in_specs=[hbm] * 7,
        out_specs=vmem,
        scratch_shapes=[
            pltpu.VMEM((2, 2 * W, W), BF16),
            pltpu.VMEM((2, 2 * W, W), BF16),
            pltpu.VMEM((W, 2 * W), BF16),
            pltpu.VMEM((4, W), F32),
            pltpu.VMEM((2, W), F32),
            pltpu.VMEM((1, 2 * W), F32),
            pltpu.VMEM((2, 2, 2 * W, 2 * W), BF16),
            pltpu.VMEM((2, 2, 8, 2 * W), F32),
            pltpu.VMEM((n_tp, 2 * W, width), BF16),
            pltpu.VMEM((2, 2, W, W), BF16),
            pltpu.VMEM((n_y, 2, W, W), BF16),
            pltpu.VMEM((2, W, W), BF16),
            pltpu.VMEM((4, 2, W, W), BF16),
            pltpu.VMEM((2, W, W), BF16),
            pltpu.VMEM((4, 2, W, W), BF16),
            pltpu.VMEM((n_y, W, 3 * W), BF16),
            pltpu.VMEM((n_y, W, W), F32),
            pltpu.VMEM((W, W), F32),
            pltpu.VMEM((2, 2, W, W), BF16),
            pltpu.VMEM((n_y, 2, W, W), BF16),
            pltpu.VMEM((n_y, W, W), BF16),
            pltpu.VMEM((2 * n_tp, W, W), BF16),
            dma((n_tp,)),
            dma((n_tp,)),
            dma,
            dma((2,)),
            dma((n_y,)),
            dma((4,)),
            dma((4,)),
            dma((4,)),
            dma((4,)),
            dma((2,)),
            dma((n_y,)),
            dma((16,)),
            dma((16,)),
            dma((8,)),
            dma((8,)),
            dma((16,)),
            dma((16,)),
            pltpu.SemaphoreType.REGULAR,
        ],
        compiler_params=pltpu.CompilerParams(collective_id=0, has_side_effects=True),
    )(
        queries,
        key_vectors,
        value_vectors,
        strengths.reshape(4, tokens),
        log_gate,
        out_gain.reshape(1, -1),
        out_weight,
    )


def solution(mesh):
    placed = (
        P("ctx", "tp"),
        P("ctx", None, "tp"),
        P("ctx", None, "tp"),
        P(None, "tp", "ctx"),
        P("tp", "ctx"),
        P("tp"),
        P("tp", None),
    )
    return jax.shard_map(
        local, mesh=mesh, in_specs=placed, out_specs=P("ctx", "tp"), check_vma=False
    )
```
